256 devices in a mesh: half: 2 (over core), cls: 2 (over y_lo), img: 64 (over y_hi, z, x).
Axes of the slice: x: 4, y: 4 (y_hi: 2, y_lo: 2; y = y_hi * 2 + y_lo), z: 8, core: 2. Of those that a mesh axis runs over, the one named last changes fastest.
Arguments:
- images: bfloat16 [2, 32768, 2, 8320], P('half', ('cls', 'img')), may hold values from -8 to 8
- projections: bfloat16 [2, 8, 8, 2, 8320], P('half', 'cls', None, None, 'img'), may hold values from -8 to 8
- ctf_table: float32 [2, 32, 8320], P('half'), may hold values from -1 to 1
- ctf_group: int32 [2, 32768], P('half', ('cls', 'img')), may hold values from 0 to 31
- orient_ids: int32 [2, 32768, 4], P('half', ('cls', 'img')), may hold values from 0 to 7
- trans_ids: int32 [2, 8], P('half'), may hold values from 0 to 24
- inv_sigma: float32 [2, 8320], P('half'), may hold values from 0.5 to 2
- counts: int32 [2, 128], P('half', ('cls', 'img')), may hold values from 1 to 256, 20480 in all within a row
Outputs:
- posterior: bfloat16 [2, 32768, 512], P('half', ('cls', 'img'))
- slab: float32 [2, 8, 8, 2, 8320], P('half', 'cls', None, None, 'img')
- fsc_map: float32 [2, 8, 8, 8320], P('half', 'cls', None, 'img')
The draws below stay inside these ranges and needn't reach their ends.
Inputs may be any that keep to these rules, and one draw needn't show every extreme that they name: counts[h, s] is the number of live particles of shard s, held in its first slots; each half-set's counts sum to 20480, and the largest is 256.
All inputs are finite; a program needn't handle non-finite values.
Results may differ from the reference program's by a relative error of at most 0.013.
The reference program's roundings to bfloat16 on the way count: a program that leaves them out, or rounds other values in their place, can miss the bound.
Values may be sent and summed in bfloat16 or wider, within the bound.
No kernel may reach another device: no remote copies, remote signals or barrier semaphores. Data moves between devices by JAX's collectives and lax.ppermute only.
A program may use at most 192 MiB of HBM per device.

```python
import math
import jax
import jax.numpy as jnp
import numpy as np
from jax import lax

K = 8
BOX = 128
FC = 8320
O = 8
TR = 8
TGRID = 5
NLOCAL = 4
G = 32
PART_DEV = 256
SHARDS = 128
PARTICLES = 32768
LIVE = 20480


ctf_square_mean = 1.0 / 3.0


inverse_mean = 1.5 / math.log(4.0)


def shared_integers(key):
    groups = jax.random.randint(jax.random.fold_in(key, 11), (2, PARTICLES), 0, G, dtype=jnp.int32)
    orients = jax.random.randint(jax.random.fold_in(key, 12), (2, PARTICLES, NLOCAL), 0, O, dtype=jnp.int32)
    shifts = jax.random.randint(jax.random.fold_in(key, 13), (2, TR), 0, TGRID * TGRID, dtype=jnp.int32)
    target_class = jax.random.randint(jax.random.fold_in(key, 14), (2, PARTICLES), 0, K, dtype=jnp.int32)
    target_slot = jax.random.randint(jax.random.fold_in(key, 15), (2, PARTICLES), 0, TR, dtype=jnp.int32)
    return (groups, orients, shifts, target_class, target_slot)


def make_ctf(key):
    return jax.random.uniform(jax.random.fold_in(key, 21), (2, G, FC), jnp.float32, -1.0, 1.0)


def make_projections(key):
    normal_part = jnp.clip(jax.random.normal(jax.random.fold_in(key, 31), (2, K, O, 2, FC), jnp.float32), -4.0, 4.0)
    target_norm = jnp.exp(jax.random.uniform(jax.random.fold_in(key, 32), (2, K, O), jnp.float32, math.log(4.0), math.log(12.0)))
    scales = jnp.sqrt(target_norm / (2.0 * FC * ctf_square_mean * inverse_mean))
    sections = normal_part * scales[:, :, :, None, None]
    return sections


def draw_images(key, part):
    groups, orients, shifts, target_class, target_slot = shared_integers(key)
    ctf_values = make_ctf(key)
    sections = make_projections(key)
    target_orient = orients[:, :, 0]
    flat_sections = sections.reshape(2, K * O, 2, FC)
    chosen = jnp.take_along_axis(flat_sections, (target_class * O + target_orient)[:, :, None, None], axis=1)
    ctf_rows = jnp.take_along_axis(ctf_values, groups[:, :, None], axis=1)
    shift_value = jnp.take_along_axis(shifts, target_slot, axis=1)
    half_width = BOX // 2 + 1
    freq_index = jnp.arange(FC, dtype=jnp.int32)
    row_index = freq_index // half_width
    wave_x = (row_index - BOX * (row_index >= BOX // 2).astype(jnp.int32)).astype(jnp.float32)
    wave_y = (freq_index % half_width).astype(jnp.float32)
    shift_x = (shift_value % TGRID - TGRID // 2).astype(jnp.float32)
    shift_y = (shift_value // TGRID - TGRID // 2).astype(jnp.float32)
    angle = 2.0 * math.pi / BOX * (shift_x[:, :, None] * wave_x[None, None, :] + shift_y[:, :, None] * wave_y[None, None, :])
    cosine = jnp.cos(angle)
    sine = jnp.sin(angle)
    real_part = chosen[:, :, 0, :]
    imag_part = chosen[:, :, 1, :]
    signal = ctf_rows[:, :, None, :] * jnp.stack([real_part * cosine - imag_part * sine, real_part * sine + imag_part * cosine], axis=2)
    noise = jnp.clip(jax.random.normal(jax.random.fold_in(key, 41), (2, PARTICLES, 2, FC), jnp.float32), -5.0, 5.0)
    return (noise + 0.5 * signal).astype(jnp.bfloat16)


def draw_projections(key, part):
    return make_projections(key).astype(jnp.bfloat16)


def draw_ctf_table(key, part):
    return make_ctf(key)


def draw_ctf_group(key, part):
    return shared_integers(key)[0]


def draw_orient_ids(key, part):
    return shared_integers(key)[1]


def draw_trans_ids(key, part):
    return shared_integers(key)[2]


def block_scale(key, dims, split, least, high):
    gain = 1.0
    for dim, parts in split:
        heights = jax.random.uniform(jax.random.fold_in(jax.random.fold_in(key, 6), dim), (parts,), jnp.float32, least / len(split), high / len(split))
        gain = gain * jnp.repeat(jnp.exp(heights), dims[dim] // parts).reshape((-1,) + (1,) * (len(dims) - 1 - dim))
    return gain


def split_up(amount, total, most, skew):
    loads = [(1 << 20) // math.isqrt(rank ** skew) + 1 for rank in range(2, amount + 1)]
    surplus, given = total - most - (amount - 1), [1] * (amount - 1)
    while surplus > 0:
        movable = [i for i in range(amount - 1) if given[i] < most]
        whole, budget = sum([loads[i] for i in movable]), surplus
        for i in movable:
            extra = min(most - given[i], max(1, budget * loads[i] // whole), surplus)
            given[i] = given[i] + extra
            surplus = surplus - extra
    return np.array([most] + given)


def uneven_parts(own_key, amount, total, most, slope):
    if amount == 2:
        one = jax.random.randint(own_key, (), max(1, total - most), min(most, total - 1) + 1)
        return jnp.stack([one, total - one])
    sizes = jnp.asarray(split_up(amount, total, most, slope), jnp.int32)
    twos = (amount - 1) // 2
    giver, receiver = sizes[1:1 + 2 * twos:2], sizes[2:2 + 2 * twos:2]
    slack = jnp.minimum(giver - 1, most - receiver)
    passed = jax.random.randint(jax.random.fold_in(own_key, 1), (twos,), 0, 1 << 20) % (slack + 1)
    sizes = sizes.at[1:1 + 2 * twos:2].set(giver - passed).at[2:2 + 2 * twos:2].set(receiver + passed)
    return sizes[jax.random.permutation(jax.random.fold_in(own_key, 2), amount)]


def setup_inputs(seed: int = 0) -> dict:
    seeds = jax.random.split(jax.random.key(seed), 9)
    images = draw_images(jax.random.fold_in(seeds[8], 71), 0)
    projections = draw_projections(jax.random.fold_in(seeds[8], 71), 0)
    ctf_table = draw_ctf_table(jax.random.fold_in(seeds[8], 71), 0)
    ctf_group = draw_ctf_group(jax.random.fold_in(seeds[8], 71), 0)
    orient_ids = draw_orient_ids(jax.random.fold_in(seeds[8], 71), 0)
    trans_ids = draw_trans_ids(jax.random.fold_in(seeds[8], 71), 0)
    inv_sigma = jnp.clip(jnp.exp(math.log(2.0) - 1.3862944 * jax.random.uniform(seeds[6], (2, FC), jnp.float32) ** block_scale(seeds[6], (2, FC), ((0, 2),), -0.2, 0.2)), 0.5, 2.0)
    counts = jax.vmap(lambda own: uneven_parts(own, SHARDS, LIVE, PART_DEV, 1))(jax.random.split(seeds[7], 2)).reshape((2, SHARDS)).astype(jnp.int32)
    return {"images": images, "projections": projections, "ctf_table": ctf_table, "ctf_group": ctf_group, "orient_ids": orient_ids, "trans_ids": trans_ids, "inv_sigma": inv_sigma, "counts": counts}


def phases(trans_list, start, count):
    half_width = BOX // 2 + 1
    freq_index = start + jnp.arange(count, dtype=jnp.int32)
    row_index = freq_index // half_width
    col_index = freq_index % half_width
    wave_x = (row_index - BOX * (row_index >= BOX // 2).astype(jnp.int32)).astype(jnp.float32)
    wave_y = col_index.astype(jnp.float32)
    shift_x = (trans_list % TGRID - TGRID // 2).astype(jnp.float32)
    shift_y = (trans_list // TGRID - TGRID // 2).astype(jnp.float32)
    angle = (2.0 * math.pi / BOX) * (shift_x[:, None] * wave_x[None, :] + shift_y[:, None] * wave_y[None, :])
    return jnp.cos(angle), jnp.sin(angle)


def shift_sections(sections, inverse, cosine, sine):
    real_part = sections[:, :, 0, :].astype(jnp.float32) * inverse
    imag_part = sections[:, :, 1, :].astype(jnp.float32) * inverse
    shifted_re = real_part[:, :, None, :] * cosine - imag_part[:, :, None, :] * sine
    shifted_im = real_part[:, :, None, :] * sine + imag_part[:, :, None, :] * cosine
    return jnp.stack([shifted_re, shifted_im], axis=3).astype(jnp.bfloat16)


def section_power(sections):
    real_part = sections[:, :, 0, :].astype(jnp.float32)
    imag_part = sections[:, :, 1, :].astype(jnp.float32)
    total = real_part * real_part + imag_part * imag_part
    return total.reshape(-1, total.shape[-1])


def contract_last(left, right):
    return lax.dot_general(left, right, (((1,), (1,)), ((), ())), preferred_element_type=jnp.float32)


def contract_high(left, right):
    return lax.dot_general(left, right, (((1,), (1,)), ((), ())), precision=lax.Precision.HIGHEST, preferred_element_type=jnp.float32)


def reference(images, projections, ctf_table, ctf_group, orient_ids, trans_ids, inv_sigma, counts):
    posts = []
    slabs = []
    for half_index in range(2):
        groups_here = ctf_group[half_index]
        ctf_rows = ctf_table[half_index][groups_here]
        weighted = (ctf_rows[:, None, :] * images[half_index].astype(jnp.float32)).astype(jnp.bfloat16)
        flat_images = weighted.reshape(PARTICLES, 2 * FC)
        cosine, sine = phases(trans_ids[half_index], 0, FC)
        inverse = inv_sigma[half_index]
        ctf_power = ctf_table[half_index] * ctf_table[half_index] * inverse

        def score_class(class_sections):
            shifted = shift_sections(class_sections[None], inverse, cosine, sine).reshape(O * TR, 2 * FC)
            cross_terms = contract_last(flat_images, shifted)
            norm_table = contract_high(ctf_power, section_power(class_sections[None]))
            return cross_terms.reshape(PARTICLES, O, TR) - 0.5 * norm_table[groups_here][:, :, None]

        scores = jnp.moveaxis(lax.map(score_class, projections[half_index]), 0, 1)
        allowed = jnp.any(orient_ids[half_index][:, :, None] == jnp.arange(O, dtype=jnp.int32)[None, None, :], axis=1)
        mask = jnp.broadcast_to(allowed[:, None, :, None], scores.shape)
        top = jnp.max(jnp.where(mask, scores, -jnp.inf), axis=(1, 2, 3), keepdims=True)
        expo = jnp.exp(jnp.where(mask, scores - top, -jnp.inf))
        total = jnp.sum(expo, axis=(1, 2, 3), keepdims=True)
        slot_index = jnp.arange(PARTICLES, dtype=jnp.int32)
        live = (slot_index % PART_DEV < counts[half_index][slot_index // PART_DEV]).astype(jnp.float32)
        weights = (expo / total * live[:, None, None, None]).astype(jnp.bfloat16)
        posts.append(weights.reshape(PARTICLES, K * O * TR))
        per_class = jnp.moveaxis(weights, 1, 0).reshape(K, PARTICLES, O * TR)

        def back_class(class_weights):
            summed = lax.dot_general(class_weights, flat_images, (((0,), (0,)), ((), ())), preferred_element_type=jnp.float32)
            summed = summed.reshape(O, TR, 2, FC)
            slab_re = jnp.sum(summed[:, :, 0] * cosine + summed[:, :, 1] * sine, axis=1)
            slab_im = jnp.sum(summed[:, :, 1] * cosine - summed[:, :, 0] * sine, axis=1)
            return jnp.stack([slab_re, slab_im], axis=1)

        slabs.append(lax.map(back_class, per_class))
    product = slabs[0][:, :, 0] * slabs[1][:, :, 0] + slabs[0][:, :, 1] * slabs[1][:, :, 1]
    return jnp.stack(posts), jnp.stack(slabs), jnp.stack([product, product])
```

```python
import math

import jax
import jax.numpy as jnp
from jax import lax
from jax.experimental import pallas as pl
from jax.experimental.pallas import tpu as pltpu
from jax.sharding import PartitionSpec as P

K = 8
BOX = 128
O = 8
TR = 8
TGRID = 5
FC = 8320
G = 32
NP = 256
LANE = 128
TILES = FC // LANE
CHUNK = 640
STEPS = FC // CHUNK
ROWS = 40
NX, NY, NZ = 4, 4, 8
PAIR = ("cls", "img")
VMEM_LIMIT = 56 * 1024 * 1024


def place(index):
    cls, img = divmod(index, 64)
    y_hi, rest = divmod(img, 32)
    z, x = divmod(rest, 4)
    return x, 2 * y_hi + cls, z


def flat(x, y, z):
    x, y, z = x % NX, y % NY, z % NZ
    return (y % 2) * 64 + (y // 2) * 32 + z * 4 + x


def send(value, dx=0, dy=0, dz=0):
    pairs = []
    for index in range(NX * NY * NZ):
        x, y, z = place(index)
        pairs.append((index, flat(x + dx, y + dy, z + dz)))
    return lax.ppermute(value, PAIR, pairs)


def fetch(value, dx=0, dy=0, dz=0):
    return send(value, -dx, -dy, -dz)


def phases(trans_list, count):
    half_width = BOX // 2 + 1
    freq_index = jnp.arange(count, dtype=jnp.int32)
    row_index = freq_index // half_width
    col_index = freq_index % half_width
    wave_x = (row_index - BOX * (row_index >= BOX // 2).astype(jnp.int32)).astype(jnp.float32)
    wave_y = col_index.astype(jnp.float32)
    shift_x = (trans_list % TGRID - TGRID // 2).astype(jnp.float32)
    shift_y = (trans_list // TGRID - TGRID // 2).astype(jnp.float32)
    angle = (
        2.0
        * math.pi
        / BOX
        * (shift_x[:, None] * wave_x[None, :] + shift_y[:, None] * wave_y[None, :])
    )
    return (jnp.cos(angle), jnp.sin(angle))


def iota(shape, dim):
    return lax.broadcasted_iota(jnp.int32, shape, dim)


def split3(value):
    high = value.astype(jnp.bfloat16)
    rest = value - high.astype(jnp.float32)
    mid = rest.astype(jnp.bfloat16)
    low = (rest - mid.astype(jnp.float32)).astype(jnp.bfloat16)
    return jnp.concatenate([high, mid, low], axis=0)


def mm(left, right, dims=((1,), (0,)), precision=None):
    return lax.dot_general(
        left, right, (dims, ((), ())), precision=precision, preferred_element_type=jnp.float32
    )


def pack_kernel(p_ref, a_ref, b_ref):
    lane = iota((8, LANE), 1)
    sub = iota((8, LANE), 0)
    for color, out in ((0, a_ref), (1, b_ref)):
        extra = jnp.zeros((8, LANE), jnp.float32)
        for kl in range(2):
            for c in range(2):
                rows = p_ref[0, color * 2 + kl, :, c, :].astype(jnp.float32)
                group = kl * 2 + c
                out[group * 8 : group * 8 + 8, :] = rows[:, :LANE].astype(jnp.bfloat16)
                first = 2 * (group * 8 + sub)
                extra += jnp.where(lane == first, rows[:, LANE : LANE + 1], 0.0)
                extra += jnp.where(lane == first + 1, rows[:, LANE + 1 : LANE + 2], 0.0)
        row = jnp.sum(extra, axis=0, keepdims=True)
        out[32:40, :] = jnp.broadcast_to(row, (8, LANE)).astype(jnp.bfloat16)


def pack_sections(projections):
    shape = jax.ShapeDtypeStruct((ROWS, LANE), jnp.bfloat16)
    return pl.pallas_call(pack_kernel, out_shape=(shape, shape), name="pack_sections")(projections)


def weight_kernel(image_ref, table_ref, group_ref, out_ref, ctf_ref):
    onehot = (group_ref[...] == iota((NP, G), 1)).astype(jnp.float32).astype(jnp.bfloat16)
    onehot3 = jnp.concatenate([onehot, onehot, onehot], axis=1)
    ctf_ref[...] = mm(onehot3, split3(table_ref[0]))

    def body(i, carry):
        rows = pl.ds(pl.multiple_of(i * 16, 16), 16)
        ctf = ctf_ref[rows, :]
        for c in range(2):
            value = image_ref[0, rows, c, :].astype(jnp.float32)
            out_ref[c, rows, :] = (ctf * value).astype(jnp.bfloat16)
        return carry

    lax.fori_loop(0, NP // 16, body, 0)


def weight_images(images, table, group_col):
    return pl.pallas_call(
        weight_kernel,
        grid=(STEPS,),
        in_specs=[
            pl.BlockSpec((1, NP, 2, CHUNK), lambda j: (0, 0, 0, j)),
            pl.BlockSpec((1, G, CHUNK), lambda j: (0, 0, j)),
            pl.BlockSpec((NP, 1), lambda j: (0, 0)),
        ],
        out_specs=pl.BlockSpec((2, NP, CHUNK), lambda j: (0, 0, j)),
        out_shape=jax.ShapeDtypeStruct((2, NP, FC), jnp.bfloat16),
        scratch_shapes=[pltpu.VMEM((NP, CHUNK), jnp.float32)],
        compiler_params=pltpu.CompilerParams(vmem_limit_bytes=VMEM_LIMIT),
        name="weight_images",
    )(images, table, group_col)


def unpack_sections(pos_ref, a_refs, b_refs, nat_ref, ex_ref):
    lane = iota((32, LANE), 1)
    mx, my, mz = pos_ref[0], pos_ref[1], pos_ref[2]
    for color, refs in ((0, a_refs), (1, b_refs)):
        for near in range(4):
            ref = refs[near]

            def body(i, carry, ref=ref, near=near, color=color):
                far, dz = i // NZ, i % NZ
                dx, dy = (near, far) if color == 0 else (far, near)
                x, y, z = (mx + dx) % NX, (my + dy) % NY, (mz + dz) % NZ
                j = (y // 2) * 32 + z * 4 + x
                base = pl.multiple_of((y % 2) * 64 + color * 32, 32)
                rows = pl.ds(base, 32)
                piece = ref[far, dz].astype(jnp.float32)
                turned = pltpu.roll(piece[:32], 2 * j, 1)
                here = pl.ds(pl.multiple_of(j * LANE, LANE), LANE)
                after = pl.ds(pl.multiple_of((j + 1) * LANE, LANE), LANE)
                nat_ref[rows, here] = jnp.where(lane >= 2 * j, turned, nat_ref[rows, here])
                nat_ref[rows, after] = jnp.where(lane < 2 * j, turned, nat_ref[rows, after])
                ex_ref[pl.ds((y % 2) * 128 + color * 64 + j, 1), :] = piece[32:33]
                return carry

            lax.fori_loop(0, 4 * NZ, body, 0)
    for cls in range(2):
        for color in range(2):
            start = cls * 128 + color * 64
            extra = ex_ref[start : start + 64, :].astype(jnp.bfloat16)
            total = jnp.zeros((32, LANE), jnp.float32)
            for u in range(2):
                pick = (iota((32, LANE), 1) == 2 * iota((32, LANE), 0) + u).astype(jnp.float32)
                column = mm(pick.astype(jnp.bfloat16), extra, ((1,), (1,)))
                spread = (iota((64, LANE), 1) == 2 * iota((64, LANE), 0) + u).astype(jnp.float32)
                total += mm(column.astype(jnp.bfloat16), spread.astype(jnp.bfloat16))
            rows = slice(cls * 64 + color * 32, cls * 64 + color * 32 + 32)
            for t in range(1, TILES):
                here = slice(t * LANE, (t + 1) * LANE)
                nat_ref[rows, here] = jnp.where(lane // 2 == t - 1, total, nat_ref[rows, here])


def score_kernel(
    pos_ref, a0, a1, a2, a3, b0, b1, b2, b3, w_ref, table_ref, inv_ref, cos_ref, sin_ref,
    group_ref, orient_ref, post_ref, left_ref, right_ref,
    nat_ref, ex_ref, shift_ref, acc_ref, norm_ref,
):
    step = pl.program_id(0)

    @pl.when(step == 0)
    def _():
        unpack_sections(pos_ref, (a0, a1, a2, a3), (b0, b1, b2, b3), nat_ref, ex_ref)
        acc_ref[...] = jnp.zeros_like(acc_ref)
        norm_ref[...] = jnp.zeros_like(norm_ref)

    table = table_ref[0]
    for tile in range(CHUNK // LANE):
        here = slice(tile * LANE, (tile + 1) * LANE)
        inverse = jnp.broadcast_to(inv_ref[0:1, here], (8, LANE))
        cosine = jnp.broadcast_to(cos_ref[:, here][:, None, :], (TR, O, LANE))
        sine = jnp.broadcast_to(sin_ref[:, here][:, None, :], (TR, O, LANE))
        place_ = pl.ds(pl.multiple_of(step * CHUNK + tile * LANE, LANE), LANE)
        for k in range(K):
            real = (nat_ref[k * 16 : k * 16 + 8, place_] * inverse)[None]
            imag = (nat_ref[k * 16 + 8 : k * 16 + 16, place_] * inverse)[None]
            rows = slice(k * 64, k * 64 + 64)
            shift_ref[0, rows, here] = (
                (real * cosine - imag * sine).reshape(TR * O, LANE).astype(jnp.bfloat16)
            )
            shift_ref[1, rows, here] = (
                (real * sine + imag * cosine).reshape(TR * O, LANE).astype(jnp.bfloat16)
            )
    lanes = pl.ds(pl.multiple_of(step * CHUNK, LANE), CHUNK)
    powers = []
    for k in range(K):
        real = nat_ref[k * 16 : k * 16 + 8, lanes]
        imag = nat_ref[k * 16 + 8 : k * 16 + 16, lanes]
        powers.append(real * real + imag * imag)
    power = jnp.concatenate(powers, axis=0)
    ctf_power = table * table * inv_ref[0:1, :]
    norm_ref[...] += mm(ctf_power, power, ((1,), (1,)), lax.Precision.HIGHEST)
    acc_ref[...] += mm(w_ref[0], shift_ref[0], ((1,), (1,))) + mm(
        w_ref[1], shift_ref[1], ((1,), (1,))
    )

    @pl.when(step == STEPS - 1)
    def _():
        wide = (K * TR * O,)
        col = iota((K * O,) + wide, 1)
        widen = (iota((K * O,) + wide, 0) == (col // (TR * O)) * O + col % O).astype(jnp.float32)
        norm_wide = mm(norm_ref[...], widen, precision=lax.Precision.HIGHEST)
        onehot = (group_ref[...] == iota((NP, G), 1)).astype(jnp.float32).astype(jnp.bfloat16)
        onehot3 = jnp.concatenate([onehot, onehot, onehot], axis=1)
        scores = acc_ref[...] - 0.5 * mm(onehot3, split3(norm_wide))
        orient = iota((NP,) + wide, 1) % O
        mask = orient_ref[:, 0:1] == orient
        for n in range(1, 4):
            mask = mask | (orient_ref[:, n : n + 1] == orient)
        top = jnp.max(jnp.where(mask, scores, -jnp.inf), axis=1, keepdims=True)
        expo = jnp.exp(jnp.where(mask, scores - top, -jnp.inf))
        total = jnp.sum(expo, axis=1, keepdims=True)
        live = (iota((NP, 1), 0) < pos_ref[3]).astype(jnp.float32)
        weights = expo / total * live
        rounded = weights.astype(jnp.bfloat16)
        row, col = iota(wide + wide, 0), iota(wide + wide, 1)
        target = (row // (TR * O)) * (TR * O) + (row % O) * TR + (row // O) % TR
        order = (col == target).astype(jnp.float32).astype(jnp.bfloat16)
        post_ref[0] = mm(rounded, order).astype(jnp.bfloat16)
        turned = weights.T.astype(jnp.bfloat16)
        for cls in range(2):
            for color, out in ((0, left_ref), (1, right_ref)):
                k = cls * 4 + color * 2
                out[cls * 128 : cls * 128 + 128, :] = turned[k * 64 : k * 64 + 128, :]


def score(pos, a, b, weighted, table, inverse, cosine, sine, group_col, orient):
    whole = pl.BlockSpec((4, NZ, ROWS, LANE), lambda j, pos: (0, 0, 0, 0))
    wide = K * O * TR
    return pl.pallas_call(
        score_kernel,
        grid_spec=pltpu.PrefetchScalarGridSpec(
            num_scalar_prefetch=1,
            grid=(STEPS,),
            in_specs=[whole] * 8
            + [
                pl.BlockSpec((2, NP, CHUNK), lambda j, pos: (0, 0, j)),
                pl.BlockSpec((1, G, CHUNK), lambda j, pos: (0, 0, j)),
                pl.BlockSpec((1, CHUNK), lambda j, pos: (0, j)),
                pl.BlockSpec((TR, CHUNK), lambda j, pos: (0, j)),
                pl.BlockSpec((TR, CHUNK), lambda j, pos: (0, j)),
                pl.BlockSpec((NP, 1), lambda j, pos: (0, 0)),
                pl.BlockSpec((NP, 4), lambda j, pos: (0, 0)),
            ],
            out_specs=[
                pl.BlockSpec((1, NP, wide), lambda j, pos: (0, 0, 0)),
                pl.BlockSpec((wide // 2, NP), lambda j, pos: (0, 0)),
                pl.BlockSpec((wide // 2, NP), lambda j, pos: (0, 0)),
            ],
            scratch_shapes=[
                pltpu.VMEM((128, FC), jnp.float32),
                pltpu.VMEM((256, LANE), jnp.float32),
                pltpu.VMEM((2, wide, CHUNK), jnp.bfloat16),
                pltpu.VMEM((NP, wide), jnp.float32),
                pltpu.VMEM((G, K * O), jnp.float32),
            ],
        ),
        out_shape=[
            jax.ShapeDtypeStruct((1, NP, wide), jnp.bfloat16),
            jax.ShapeDtypeStruct((wide // 2, NP), jnp.bfloat16),
            jax.ShapeDtypeStruct((wide // 2, NP), jnp.bfloat16),
        ],
        compiler_params=pltpu.CompilerParams(vmem_limit_bytes=VMEM_LIMIT),
        name="score",
    )(pos, *a, *b, weighted, table, inverse, cosine, sine, group_col, orient)


def back_kernel(
    color, pos_ref, post_ref, w_ref, cos_ref, sin_ref, p0, p1, p2, p3,
    slab_ref, re_ref, im_ref, ex_ref,
):
    step = pl.program_id(0)
    re_ref[...] = mm(post_ref[...], w_ref[0])
    im_ref[...] = mm(post_ref[...], w_ref[1])
    for tile in range(CHUNK // LANE):
        here = slice(tile * LANE, (tile + 1) * LANE)
        cosine = jnp.broadcast_to(cos_ref[:, here][:, None, :], (TR, O, LANE))
        sine = jnp.broadcast_to(sin_ref[:, here][:, None, :], (TR, O, LANE))
        place_ = pl.ds(pl.multiple_of(step * CHUNK + tile * LANE, LANE), LANE)
        for k in range(4):
            rows = slice(k * 64, k * 64 + 64)
            real = re_ref[rows, here].reshape(TR, O, LANE)
            imag = im_ref[rows, here].reshape(TR, O, LANE)
            slab_ref[k * 16 : k * 16 + 8, place_] = jnp.sum(real * cosine + imag * sine, axis=0)
            slab_ref[k * 16 + 8 : k * 16 + 16, place_] = jnp.sum(
                imag * cosine - real * sine, axis=0
            )

    @pl.when(step == STEPS - 1)
    def _():
        lane = iota((32, LANE), 1)
        for cls in range(2):
            rows = slice(cls * 32, cls * 32 + 32)
            tails = jnp.zeros((32, LANE), jnp.float32)
            for t in range(1, TILES):
                tails = jnp.where(
                    lane // 2 == t - 1, slab_ref[rows, t * LANE : (t + 1) * LANE], tails
                )
            tails = tails.astype(jnp.bfloat16)
            total = jnp.zeros((64, LANE), jnp.float32)
            for u in range(2):
                pick = (iota((64, LANE), 1) == 2 * iota((64, LANE), 0) + u).astype(jnp.float32)
                column = mm(pick.astype(jnp.bfloat16), tails, ((1,), (1,)))
                spread = (iota((32, LANE), 1) == 2 * iota((32, LANE), 0) + u).astype(jnp.float32)
                total += mm(column.astype(jnp.bfloat16), spread.astype(jnp.bfloat16))
            ex_ref[cls * 64 : cls * 64 + 64, :] = total
        mx, my, mz = pos_ref[0], pos_ref[1], pos_ref[2]
        for near, out in enumerate((p0, p1, p2, p3)):

            def body(i, carry, near=near, out=out):
                far, dz = i // NZ, i % NZ
                dx, dy = (near, far) if color == 0 else (far, near)
                x, y, z = (mx + dx) % NX, (my + dy) % NY, (mz + dz) % NZ
                j = (y // 2) * 32 + z * 4 + x
                rows = pl.ds(pl.multiple_of((y % 2) * 32, 32), 32)
                here = pl.ds(pl.multiple_of(j * LANE, LANE), LANE)
                after = pl.ds(pl.multiple_of((j + 1) * LANE, LANE), LANE)
                both = jnp.where(lane >= 2 * j, slab_ref[rows, here], slab_ref[rows, after])
                main = pltpu.roll(both, LANE - 2 * j, 1)
                tail = ex_ref[pl.ds((y % 2) * 64 + j, 1), :]
                out[far, dz, 0:32, :] = main.astype(jnp.bfloat16)
                out[far, dz, 32:40, :] = jnp.broadcast_to(tail, (8, LANE)).astype(jnp.bfloat16)
                return carry

            lax.fori_loop(0, 4 * NZ, body, 0)


def project_back(color, pos, post, weighted, cosine, sine):
    whole = pl.BlockSpec((4, NZ, ROWS, LANE), lambda j, pos: (0, 0, 0, 0))

    def kernel(*refs):
        back_kernel(color, *refs)

    return pl.pallas_call(
        kernel,
        grid_spec=pltpu.PrefetchScalarGridSpec(
            num_scalar_prefetch=1,
            grid=(STEPS,),
            in_specs=[
                pl.BlockSpec((NP, NP), lambda j, pos: (0, 0)),
                pl.BlockSpec((2, NP, CHUNK), lambda j, pos: (0, 0, j)),
                pl.BlockSpec((TR, CHUNK), lambda j, pos: (0, j)),
                pl.BlockSpec((TR, CHUNK), lambda j, pos: (0, j)),
            ],
            out_specs=[whole] * 4,
            scratch_shapes=[
                pltpu.VMEM((64, FC), jnp.float32),
                pltpu.VMEM((NP, CHUNK), jnp.float32),
                pltpu.VMEM((NP, CHUNK), jnp.float32),
                pltpu.VMEM((128, LANE), jnp.float32),
            ],
        ),
        out_shape=[jax.ShapeDtypeStruct((4, NZ, ROWS, LANE), jnp.bfloat16)] * 4,
        compiler_params=pltpu.CompilerParams(vmem_limit_bytes=VMEM_LIMIT),
        name="project_back_" + str(color),
    )(pos, post, weighted, cosine, sine)


def finish_kernel(own_ref, partner_ref, slab_ref, product_ref):
    lane = iota((8, LANE), 1)
    sub = iota((8, LANE), 0)

    def tails(row, group):
        first = 2 * (group * 8 + sub)
        wide = jnp.broadcast_to(row, (8, LANE))
        one = jnp.sum(jnp.where(lane == first, wide, 0.0), axis=1, keepdims=True)
        two = jnp.sum(jnp.where(lane == first + 1, wide, 0.0), axis=1, keepdims=True)
        return jnp.concatenate([one, two], axis=1)

    for color in range(2):
        base = color * ROWS
        own_row = own_ref[base + 32 : base + 33, :]
        partner_row = partner_ref[base + 32 : base + 40, :].astype(jnp.float32)[0:1]
        for kl in range(2):
            k = color * 2 + kl
            main, edge = 0.0, 0.0
            for c in range(2):
                group = kl * 2 + c
                rows = slice(base + group * 8, base + group * 8 + 8)
                own = own_ref[rows, :]
                own_tail = tails(own_row, group)
                slab_ref[0, k, :, c, 0:LANE] = own
                slab_ref[0, k, :, c, LANE : LANE + 2] = own_tail
                main += own * partner_ref[rows, :].astype(jnp.float32)
                edge += own_tail * tails(partner_row, group)
            product_ref[0, k, :, 0:LANE] = main
            product_ref[0, k, :, LANE : LANE + 2] = edge


def finish(own, partner):
    return pl.pallas_call(
        finish_kernel,
        out_shape=(
            jax.ShapeDtypeStruct((1, 4, O, 2, 130), jnp.float32),
            jax.ShapeDtypeStruct((1, 4, O, 130), jnp.float32),
        ),
        name="finish",
    )(own, partner)


def added(parts):
    total = parts[0].astype(jnp.float32)
    for part in parts[1:]:
        total = total + part.astype(jnp.float32)
    return total


def on_device(images, projections, ctf_table, ctf_group, orient_ids, trans_ids, inv_sigma, counts):
    cls, img = lax.axis_index("cls"), lax.axis_index("img")
    pos = jnp.stack(
        [img % 4, 2 * (img // 32) + cls, (img // 4) % 8, counts[0, 0]]
    ).astype(jnp.int32)
    group_col = ctf_group[0][:, None]

    left, right = pack_sections(projections)
    shard = jnp.concatenate([left, right], axis=0)
    along = jnp.stack([shard] + [fetch(shard, dz=d) for d in range(1, NZ)])
    left, right = along[:, :ROWS], along[:, ROWS:]
    left = jnp.stack([left] + [fetch(left, dy=d) for d in range(1, NY)])
    right = jnp.stack([right] + [fetch(right, dx=d) for d in range(1, NX)])
    lefts = [left] + [fetch(left, dx=d) for d in range(1, NX)]
    rights = [right] + [fetch(right, dy=d) for d in range(1, NY)]

    cosine, sine = phases(trans_ids[0], FC)
    weighted = weight_images(images, ctf_table, group_col)
    posterior, post_left, post_right = score(
        pos, lefts, rights, weighted, ctf_table, inv_sigma, cosine, sine, group_col, orient_ids[0]
    )

    pieces = project_back(0, pos, post_left, weighted, cosine, sine)
    left = added([pieces[0]] + [send(pieces[d], dx=d) for d in range(1, NX)])
    pieces = project_back(1, pos, post_right, weighted, cosine, sine)
    right = added([pieces[0]] + [send(pieces[d], dy=d) for d in range(1, NY)])
    left, right = left.astype(jnp.bfloat16), right.astype(jnp.bfloat16)
    left = added([left[0]] + [send(left[d], dy=d) for d in range(1, NY)])
    right = added([right[0]] + [send(right[d], dx=d) for d in range(1, NX)])
    both = jnp.concatenate([left, right], axis=1).astype(jnp.bfloat16)
    own = added([both[0]] + [send(both[d], dz=d) for d in range(1, NZ)])
    partner = lax.ppermute(own.astype(jnp.bfloat16), "half", [(0, 1), (1, 0)])
    slab, product = finish(own, partner)
    return (posterior, slab, product)


def solution(mesh):
    return jax.shard_map(
        on_device,
        mesh=mesh,
        in_specs=(
            P("half", ("cls", "img"), None, None),
            P("half", "cls", None, None, "img"),
            P("half", None, None),
            P("half", ("cls", "img")),
            P("half", ("cls", "img"), None),
            P("half", None),
            P("half", None),
            P("half", ("cls", "img")),
        ),
        out_specs=(
            P("half", ("cls", "img"), None),
            P("half", "cls", None, None, "img"),
            P("half", "cls", None, "img"),
        ),
        check_vma=False,
    )
```

```python
import math

import jax
import jax.numpy as jnp
from jax import lax
from jax.experimental import pallas as pl
from jax.experimental.pallas import tpu as pltpu
from jax.sharding import PartitionSpec as P

K = 8
BOX = 128
O = 8
TR = 8
TGRID = 5
FC = 8320
G = 32
NP = 256
LANE = 128
TILES = FC // LANE
CHUNK = 1664
STEPS = FC // CHUNK
ROWS = 40
NX, NY, NZ = 4, 4, 8
Z_ORDER = (0, 4, 1, 5, 2, 6, 7, 3)
PAIR = ("cls", "img")
VMEM_LIMIT = 56 * 1024 * 1024


def place(index):
    cls, img = divmod(index, 64)
    y_hi, rest = divmod(img, 32)
    z, x = divmod(rest, 4)
    return x, 2 * y_hi + cls, z


def flat(x, y, z):
    x, y, z = x % NX, y % NY, z % NZ
    return (y % 2) * 64 + (y // 2) * 32 + z * 4 + x


def send(value, dx=0, dy=0, dz=0):
    pairs = []
    for index in range(NX * NY * NZ):
        x, y, z = place(index)
        pairs.append((index, flat(x + dx, y + dy, z + dz)))
    return lax.ppermute(value, PAIR, pairs)


def fetch(value, dx=0, dy=0, dz=0):
    return send(value, -dx, -dy, -dz)


def phases(trans_list, count):
    half_width = BOX // 2 + 1
    freq_index = jnp.arange(count, dtype=jnp.int32)
    row_index = freq_index // half_width
    col_index = freq_index % half_width
    wave_x = (row_index - BOX * (row_index >= BOX // 2).astype(jnp.int32)).astype(jnp.float32)
    wave_y = col_index.astype(jnp.float32)
    shift_x = (trans_list % TGRID - TGRID // 2).astype(jnp.float32)
    shift_y = (trans_list // TGRID - TGRID // 2).astype(jnp.float32)
    angle = (
        2.0
        * math.pi
        / BOX
        * (shift_x[:, None] * wave_x[None, :] + shift_y[:, None] * wave_y[None, :])
    )
    return (jnp.cos(angle), jnp.sin(angle))


def iota(shape, dim):
    return lax.broadcasted_iota(jnp.int32, shape, dim)


def split3(value, axis=0):
    high = value.astype(jnp.bfloat16)
    rest = value - high.astype(jnp.float32)
    mid = rest.astype(jnp.bfloat16)
    low = (rest - mid.astype(jnp.float32)).astype(jnp.bfloat16)
    return jnp.concatenate([high, mid, low], axis=axis)


def mm(left, right, dims=((1,), (0,)), precision=None):
    return lax.dot_general(
        left, right, (dims, ((), ())), precision=precision, preferred_element_type=jnp.float32
    )


def pack_kernel(p_ref, a_ref, b_ref):
    lane = iota((8, LANE), 1)
    sub = iota((8, LANE), 0)
    for color, out in ((0, a_ref), (1, b_ref)):
        extra = jnp.zeros((8, LANE), jnp.float32)
        for kl in range(2):
            for c in range(2):
                rows = p_ref[0, color * 2 + kl, :, c, :].astype(jnp.float32)
                group = kl * 2 + c
                out[group * 8 : group * 8 + 8, :] = rows[:, :LANE].astype(jnp.bfloat16)
                first = 2 * (group * 8 + sub)
                extra += jnp.where(lane == first, rows[:, LANE : LANE + 1], 0.0)
                extra += jnp.where(lane == first + 1, rows[:, LANE + 1 : LANE + 2], 0.0)
        row = jnp.sum(extra, axis=0, keepdims=True)
        out[32:40, :] = jnp.broadcast_to(row, (8, LANE)).astype(jnp.bfloat16)


def pack_sections(projections):
    shape = jax.ShapeDtypeStruct((ROWS, LANE), jnp.bfloat16)
    return pl.pallas_call(pack_kernel, out_shape=(shape, shape), name="pack_sections")(projections)


def onehot_rows(group_row):
    onehot = (iota((G, NP), 0) == group_row).astype(jnp.float32)
    return jnp.concatenate([onehot, onehot, onehot], axis=0)


def weight_kernel(image_ref, table_ref, group_ref, out_ref, ctf_ref, onehot_ref):
    @pl.when(pl.program_id(0) == 0)
    def _():
        onehot_ref[...] = onehot_rows(group_ref[...]).T.astype(jnp.bfloat16)

    ctf_ref[...] = mm(onehot_ref[...], split3(table_ref[0]))

    def body(i, carry):
        rows = pl.ds(pl.multiple_of(i * 16, 16), 16)
        ctf = ctf_ref[rows, :]
        for c in range(2):
            value = image_ref[0, rows, c, :].astype(jnp.float32)
            out_ref[c, rows, :] = (ctf * value).astype(jnp.bfloat16)
        return carry

    lax.fori_loop(0, NP // 16, body, 0)


def weight_images(images, table, group_row):
    return pl.pallas_call(
        weight_kernel,
        grid=(STEPS,),
        in_specs=[
            pl.BlockSpec((1, NP, 2, CHUNK), lambda j: (0, 0, 0, j)),
            pl.BlockSpec((1, G, CHUNK), lambda j: (0, 0, j)),
            pl.BlockSpec((1, NP), lambda j: (0, 0)),
        ],
        out_specs=pl.BlockSpec((2, NP, CHUNK), lambda j: (0, 0, j)),
        out_shape=jax.ShapeDtypeStruct((2, NP, FC), jnp.bfloat16),
        scratch_shapes=[
            pltpu.VMEM((NP, CHUNK), jnp.float32),
            pltpu.VMEM((NP, 3 * G), jnp.bfloat16),
        ],
        compiler_params=pltpu.CompilerParams(vmem_limit_bytes=VMEM_LIMIT),
        name="weight_images",
    )(images, table, group_row)


def unpack_sections(pos_ref, a_refs, b_refs, nat_ref, ex_ref):
    lane = iota((32, LANE), 1)
    mx, my, mz = pos_ref[0], pos_ref[1], pos_ref[2]
    for color, refs in ((0, a_refs), (1, b_refs)):
        for near in range(4):
            ref = refs[near]

            def body(far, carry, ref=ref, near=near, color=color):
                dx, dy = (near, far) if color == 0 else (far, near)
                x, y = (mx + dx) % NX, (my + dy) % NY
                rows = pl.ds(pl.multiple_of((y % 2) * 64 + color * 32, 32), 32)
                for slot, dz in enumerate(Z_ORDER):
                    j = (y // 2) * 32 + ((mz + dz) % NZ) * 4 + x
                    piece = ref[far, slot].astype(jnp.float32)
                    turned = pltpu.roll(piece[:32], 2 * j, 1)
                    here = pl.ds(pl.multiple_of(j * LANE, LANE), LANE)
                    after = pl.ds(pl.multiple_of((j + 1) * LANE, LANE), LANE)
                    pltpu.store(nat_ref.at[rows, here], turned, mask=lane >= 2 * j)
                    pltpu.store(nat_ref.at[rows, after], turned, mask=lane < 2 * j)
                    ex_ref[pl.ds((y % 2) * 128 + color * 64 + j, 1), :] = piece[32:33]
                return carry

            lax.fori_loop(0, 4, body, 0)
    for cls in range(2):
        for color in range(2):
            start = cls * 128 + color * 64
            extra = ex_ref[start : start + 64, :].astype(jnp.bfloat16)
            total = jnp.zeros((32, LANE), jnp.float32)
            for u in range(2):
                pick = (iota((32, LANE), 1) == 2 * iota((32, LANE), 0) + u).astype(jnp.float32)
                column = mm(pick.astype(jnp.bfloat16), extra, ((1,), (1,)))
                spread = (iota((64, LANE), 1) == 2 * iota((64, LANE), 0) + u).astype(jnp.float32)
                total += mm(column.astype(jnp.bfloat16), spread.astype(jnp.bfloat16))
            rows = slice(cls * 64 + color * 32, cls * 64 + color * 32 + 32)
            for t in range(1, TILES):
                here = slice(t * LANE, (t + 1) * LANE)
                pltpu.store(nat_ref.at[rows, here], total, mask=lane // 2 == t - 1)


def score_kernel(
    pos_ref, a0, a1, a2, a3, b0, b1, b2, b3, w_ref, table_ref, inv_ref, cos_ref, sin_ref,
    group_ref, orient_ref, post_ref, left_ref, right_ref,
    nat_ref, ex_ref, shift_ref, acc_ref, norm_ref,
):
    step = pl.program_id(0)

    @pl.when(step == 0)
    def _():
        unpack_sections(pos_ref, (a0, a1, a2, a3), (b0, b1, b2, b3), nat_ref, ex_ref)
        acc_ref[...] = jnp.zeros_like(acc_ref)
        norm_ref[...] = jnp.zeros_like(norm_ref)

    def body(tile, carry):
        here = pl.ds(pl.multiple_of(tile * LANE, LANE), LANE)
        inverse = jnp.broadcast_to(inv_ref[0:1, here], (8, LANE))
        cosine = jnp.broadcast_to(cos_ref[:, here][:, None, :], (TR, O, LANE))
        sine = jnp.broadcast_to(sin_ref[:, here][:, None, :], (TR, O, LANE))
        place_ = pl.ds(pl.multiple_of(step * CHUNK + tile * LANE, LANE), LANE)
        for k in range(K):
            real = (nat_ref[k * 16 : k * 16 + 8, place_] * inverse)[None]
            imag = (nat_ref[k * 16 + 8 : k * 16 + 16, place_] * inverse)[None]
            rows = slice(k * 64, k * 64 + 64)
            shift_ref[0, rows, here] = (
                (real * cosine - imag * sine).reshape(TR * O, LANE).astype(jnp.bfloat16)
            )
            shift_ref[1, rows, here] = (
                (real * sine + imag * cosine).reshape(TR * O, LANE).astype(jnp.bfloat16)
            )
        return carry

    lax.fori_loop(0, CHUNK // LANE, body, 0)
    table = table_ref[0]
    lanes = pl.ds(pl.multiple_of(step * CHUNK, LANE), CHUNK)
    powers = []
    for k in range(K):
        real = nat_ref[k * 16 : k * 16 + 8, lanes]
        imag = nat_ref[k * 16 + 8 : k * 16 + 16, lanes]
        powers.append(real * real + imag * imag)
    power = jnp.concatenate(powers, axis=0)
    ctf_power = table * table * inv_ref[0:1, :]
    norm_ref[...] += mm(power, ctf_power, ((1,), (1,)), lax.Precision.HIGHEST)
    acc_ref[...] += mm(shift_ref[0], w_ref[0], ((1,), (1,))) + mm(
        shift_ref[1], w_ref[1], ((1,), (1,))
    )

    @pl.when(step == STEPS - 1)
    def _():
        wide = K * TR * O
        row = iota((wide, K * O), 0)
        widen = (iota((wide, K * O), 1) == (row // (TR * O)) * O + row % O).astype(jnp.float32)
        norm_wide = mm(widen, norm_ref[...], precision=lax.Precision.HIGHEST)
        onehot3 = onehot_rows(group_ref[...]).astype(jnp.bfloat16)
        scores = acc_ref[...] - 0.5 * mm(split3(norm_wide, 1), onehot3)
        orient = iota((wide, NP), 0) % O
        mask = orient_ref[0:1, :] == orient
        for n in range(1, 4):
            mask = mask | (orient_ref[n : n + 1, :] == orient)
        top = jnp.max(jnp.where(mask, scores, -jnp.inf), axis=0, keepdims=True)
        expo = jnp.exp(jnp.where(mask, scores - top, -jnp.inf))
        total = jnp.sum(expo, axis=0, keepdims=True)
        live = (iota((1, NP), 1) < pos_ref[3]).astype(jnp.float32)
        weights = expo / total * live
        rounded = weights.astype(jnp.bfloat16)
        for cls in range(2):
            for color, out in ((0, left_ref), (1, right_ref)):
                k = cls * 4 + color * 2
                out[cls * 128 : cls * 128 + 128, :] = rounded[k * 64 : k * 64 + 128, :]
        row, col = iota((wide, wide), 0), iota((wide, wide), 1)
        target = (row // (TR * O)) * (TR * O) + (row % O) * TR + (row // O) % TR
        order = (col == target).astype(jnp.float32).astype(jnp.bfloat16)
        post_ref[0] = mm(weights.T.astype(jnp.bfloat16), order).astype(jnp.bfloat16)


def score(pos, a, b, weighted, table, inverse, cosine, sine, group_row, orient):
    whole = pl.BlockSpec((4, NZ, ROWS, LANE), lambda j, pos: (0, 0, 0, 0))
    wide = K * O * TR
    return pl.pallas_call(
        score_kernel,
        grid_spec=pltpu.PrefetchScalarGridSpec(
            num_scalar_prefetch=1,
            grid=(STEPS,),
            in_specs=[whole] * 8
            + [
                pl.BlockSpec((2, NP, CHUNK), lambda j, pos: (0, 0, j)),
                pl.BlockSpec((1, G, CHUNK), lambda j, pos: (0, 0, j)),
                pl.BlockSpec((1, CHUNK), lambda j, pos: (0, j)),
                pl.BlockSpec((TR, CHUNK), lambda j, pos: (0, j)),
                pl.BlockSpec((TR, CHUNK), lambda j, pos: (0, j)),
                pl.BlockSpec((1, NP), lambda j, pos: (0, 0)),
                pl.BlockSpec((4, NP), lambda j, pos: (0, 0)),
            ],
            out_specs=[
                pl.BlockSpec((1, NP, wide), lambda j, pos: (0, 0, 0)),
                pl.BlockSpec((wide // 2, NP), lambda j, pos: (0, 0)),
                pl.BlockSpec((wide // 2, NP), lambda j, pos: (0, 0)),
            ],
            scratch_shapes=[
                pltpu.VMEM((128, FC), jnp.float32),
                pltpu.VMEM((256, LANE), jnp.float32),
                pltpu.VMEM((2, wide, CHUNK), jnp.bfloat16),
                pltpu.VMEM((wide, NP), jnp.float32),
                pltpu.VMEM((K * O, G), jnp.float32),
            ],
        ),
        out_shape=[
            jax.ShapeDtypeStruct((1, NP, wide), jnp.bfloat16),
            jax.ShapeDtypeStruct((wide // 2, NP), jnp.bfloat16),
            jax.ShapeDtypeStruct((wide // 2, NP), jnp.bfloat16),
        ],
        compiler_params=pltpu.CompilerParams(vmem_limit_bytes=VMEM_LIMIT),
        name="score",
    )(pos, *a, *b, weighted, table, inverse, cosine, sine, group_row, orient)


def back_kernel(
    color, pos_ref, post_ref, w_ref, cos_ref, sin_ref, p0, p1, p2, p3,
    slab_ref, re_ref, im_ref, ex_ref,
):
    step = pl.program_id(0)
    re_ref[...] = mm(post_ref[...], w_ref[0])
    im_ref[...] = mm(post_ref[...], w_ref[1])

    def combine(tile, carry):
        here = pl.ds(pl.multiple_of(tile * LANE, LANE), LANE)
        cosine = jnp.broadcast_to(cos_ref[:, here][:, None, :], (TR, O, LANE))
        sine = jnp.broadcast_to(sin_ref[:, here][:, None, :], (TR, O, LANE))
        place_ = pl.ds(pl.multiple_of(step * CHUNK + tile * LANE, LANE), LANE)
        for k in range(4):
            rows = slice(k * 64, k * 64 + 64)
            real = re_ref[rows, here].reshape(TR, O, LANE)
            imag = im_ref[rows, here].reshape(TR, O, LANE)
            slab_ref[k * 16 : k * 16 + 8, place_] = jnp.sum(real * cosine + imag * sine, axis=0)
            slab_ref[k * 16 + 8 : k * 16 + 16, place_] = jnp.sum(
                imag * cosine - real * sine, axis=0
            )
        return carry

    lax.fori_loop(0, CHUNK // LANE, combine, 0)

    @pl.when(step == STEPS - 1)
    def _():
        lane = iota((32, LANE), 1)
        for cls in range(2):
            rows = slice(cls * 32, cls * 32 + 32)
            tails = jnp.zeros((32, LANE), jnp.float32)
            for t in range(1, TILES):
                tails = jnp.where(
                    lane // 2 == t - 1, slab_ref[rows, t * LANE : (t + 1) * LANE], tails
                )
            tails = tails.astype(jnp.bfloat16)
            total = jnp.zeros((64, LANE), jnp.float32)
            for u in range(2):
                pick = (iota((64, LANE), 1) == 2 * iota((64, LANE), 0) + u).astype(jnp.float32)
                column = mm(pick.astype(jnp.bfloat16), tails, ((1,), (1,)))
                spread = (iota((32, LANE), 1) == 2 * iota((32, LANE), 0) + u).astype(jnp.float32)
                total += mm(column.astype(jnp.bfloat16), spread.astype(jnp.bfloat16))
            ex_ref[cls * 64 : cls * 64 + 64, :] = total
        mx, my, mz = pos_ref[0], pos_ref[1], pos_ref[2]
        for near, out in enumerate((p0, p1, p2, p3)):

            def body(far, carry, near=near, out=out):
                dx, dy = (near, far) if color == 0 else (far, near)
                x, y = (mx + dx) % NX, (my + dy) % NY
                rows = pl.ds(pl.multiple_of((y % 2) * 32, 32), 32)
                for slot, dz in enumerate(Z_ORDER):
                    j = (y // 2) * 32 + ((mz + dz) % NZ) * 4 + x
                    here = pl.ds(pl.multiple_of(j * LANE, LANE), LANE)
                    after = pl.ds(pl.multiple_of((j + 1) * LANE, LANE), LANE)
                    both = jnp.where(lane >= 2 * j, slab_ref[rows, here], slab_ref[rows, after])
                    main = pltpu.roll(both, LANE - 2 * j, 1)
                    tail = ex_ref[pl.ds((y % 2) * 64 + j, 1), :]
                    out[far, slot, 0:32, :] = main.astype(jnp.bfloat16)
                    out[far, slot, 32:40, :] = jnp.broadcast_to(tail, (8, LANE)).astype(
                        jnp.bfloat16
                    )
                return carry

            lax.fori_loop(0, 4, body, 0)


def project_back(color, pos, post, weighted, cosine, sine):
    whole = pl.BlockSpec((4, NZ, ROWS, LANE), lambda j, pos: (0, 0, 0, 0))

    def kernel(*refs):
        back_kernel(color, *refs)

    return pl.pallas_call(
        kernel,
        grid_spec=pltpu.PrefetchScalarGridSpec(
            num_scalar_prefetch=1,
            grid=(STEPS,),
            in_specs=[
                pl.BlockSpec((NP, NP), lambda j, pos: (0, 0)),
                pl.BlockSpec((2, NP, CHUNK), lambda j, pos: (0, 0, j)),
                pl.BlockSpec((TR, CHUNK), lambda j, pos: (0, j)),
                pl.BlockSpec((TR, CHUNK), lambda j, pos: (0, j)),
            ],
            out_specs=[whole] * 4,
            scratch_shapes=[
                pltpu.VMEM((64, FC), jnp.float32),
                pltpu.VMEM((NP, CHUNK), jnp.float32),
                pltpu.VMEM((NP, CHUNK), jnp.float32),
                pltpu.VMEM((128, LANE), jnp.float32),
            ],
        ),
        out_shape=[jax.ShapeDtypeStruct((4, NZ, ROWS, LANE), jnp.bfloat16)] * 4,
        compiler_params=pltpu.CompilerParams(vmem_limit_bytes=VMEM_LIMIT),
        name="project_back_" + str(color),
    )(pos, post, weighted, cosine, sine)


def finish_kernel(own_ref, partner_ref, slab_ref, product_ref):
    lane = iota((8, LANE), 1)
    sub = iota((8, LANE), 0)

    def tails(row, group):
        first = 2 * (group * 8 + sub)
        wide = jnp.broadcast_to(row, (8, LANE))
        one = jnp.sum(jnp.where(lane == first, wide, 0.0), axis=1, keepdims=True)
        two = jnp.sum(jnp.where(lane == first + 1, wide, 0.0), axis=1, keepdims=True)
        return jnp.concatenate([one, two], axis=1)

    for color in range(2):
        base = color * ROWS
        own_row = own_ref[base + 32 : base + 33, :]
        partner_row = partner_ref[base + 32 : base + 40, :].astype(jnp.float32)[0:1]
        for kl in range(2):
            k = color * 2 + kl
            main, edge = 0.0, 0.0
            for c in range(2):
                group = kl * 2 + c
                rows = slice(base + group * 8, base + group * 8 + 8)
                own = own_ref[rows, :]
                own_tail = tails(own_row, group)
                slab_ref[0, k, :, c, 0:LANE] = own
                slab_ref[0, k, :, c, LANE : LANE + 2] = own_tail
                main += own * partner_ref[rows, :].astype(jnp.float32)
                edge += own_tail * tails(partner_row, group)
            product_ref[0, k, :, 0:LANE] = main
            product_ref[0, k, :, LANE : LANE + 2] = edge


def finish(own, partner):
    return pl.pallas_call(
        finish_kernel,
        out_shape=(
            jax.ShapeDtypeStruct((1, 4, O, 2, 130), jnp.float32),
            jax.ShapeDtypeStruct((1, 4, O, 130), jnp.float32),
        ),
        name="finish",
    )(own, partner)


def added(parts):
    total = parts[0].astype(jnp.float32)
    for part in parts[1:]:
        total = total + part.astype(jnp.float32)
    return total


def on_device(images, projections, ctf_table, ctf_group, orient_ids, trans_ids, inv_sigma, counts):
    cls, img = lax.axis_index("cls"), lax.axis_index("img")
    pos = jnp.stack(
        [img % 4, 2 * (img // 32) + cls, (img // 4) % 8, counts[0, 0]]
    ).astype(jnp.int32)
    group_row = ctf_group

    left, right = pack_sections(projections)
    shard = jnp.concatenate([left, right], axis=0)
    along = jnp.stack([shard, fetch(shard, dz=4)])
    along = jnp.concatenate([along] + [fetch(along, dz=d) for d in (1, 2, -1)])
    left, right = along[:, :ROWS], along[:, ROWS:]
    left = jnp.stack([left] + [fetch(left, dy=d) for d in range(1, NY)])
    right = jnp.stack([right] + [fetch(right, dx=d) for d in range(1, NX)])
    lefts = [left] + [fetch(left, dx=d) for d in range(1, NX)]
    rights = [right] + [fetch(right, dy=d) for d in range(1, NY)]

    cosine, sine = phases(trans_ids[0], FC)
    weighted = weight_images(images, ctf_table, group_row)
    posterior, post_left, post_right = score(
        pos, lefts, rights, weighted, ctf_table, inv_sigma, cosine, sine, group_row, orient_ids[0].T
    )

    pieces = project_back(0, pos, post_left, weighted, cosine, sine)
    left = added([pieces[0]] + [send(pieces[d], dx=d) for d in range(1, NX)])
    pieces = project_back(1, pos, post_right, weighted, cosine, sine)
    right = added([pieces[0]] + [send(pieces[d], dy=d) for d in range(1, NY)])
    left, right = left.astype(jnp.bfloat16), right.astype(jnp.bfloat16)
    left = added([left[0]] + [send(left[d], dy=d) for d in range(1, NY)])
    right = added([right[0]] + [send(right[d], dx=d) for d in range(1, NX)])
    both = jnp.concatenate([left, right], axis=1).astype(jnp.bfloat16)
    parts = [both[0:2]] + [send(both[2 * n : 2 * n + 2], dz=d) for n, d in ((1, 1), (2, 2), (3, -1))]
    pair = added(parts)
    own = pair[0] + send(pair[1], dz=4)
    partner = lax.ppermute(own.astype(jnp.bfloat16), "half", [(0, 1), (1, 0)])
    slab, product = finish(own, partner)
    return (posterior, slab, product)


def solution(mesh):
    return jax.shard_map(
        on_device,
        mesh=mesh,
        in_specs=(
            P("half", ("cls", "img"), None, None),
            P("half", "cls", None, None, "img"),
            P("half", None, None),
            P("half", ("cls", "img")),
            P("half", ("cls", "img"), None),
            P("half", None),
            P("half", None),
            P("half", ("cls", "img")),
        ),
        out_specs=(
            P("half", ("cls", "img"), None),
            P("half", "cls", None, None, "img"),
            P("half", "cls", None, "img"),
        ),
        check_vma=False,
    )
```

```python
import math

import jax
import jax.numpy as jnp
from jax import lax
from jax.experimental import pallas as pl
from jax.experimental.pallas import tpu as pltpu
from jax.sharding import PartitionSpec as P

K = 8
BOX = 128
O = 8
TR = 8
TGRID = 5
FC = 8320
G = 32
NP = 256
LANE = 128
TILES = FC // LANE
CHUNK = 640
STEPS = FC // CHUNK
PART = 1664
ROWS = 40
NX, NY, NZ = 4, 4, 8
GRAY = (0, 1, 3, 2)
Z_ORDER = (0, -1, 1, 2, -3, -2, -4, -5)
PAIR = ("cls", "img")
VMEM_LIMIT = 56 * 1024 * 1024


def place(index):
    cls, img = divmod(index, 64)
    y_hi, rest = divmod(img, 32)
    z, x = divmod(rest, 4)
    return x, 2 * y_hi + cls, z


def flat(x, y, z):
    x, y, z = x % NX, y % NY, z % NZ
    return (y % 2) * 64 + (y // 2) * 32 + z * 4 + x


def trade(value, mx=0, my=0):
    pairs = []
    for index in range(NX * NY * NZ):
        x, y, z = place(index)
        pairs.append((index, flat(x ^ mx, y ^ my, z)))
    return lax.ppermute(value, PAIR, pairs)


def trade_z(value, odd):
    pairs = []
    for index in range(NX * NY * NZ):
        x, y, z = place(index)
        pairs.append((index, flat(x, y, z + odd if z % 2 else z - odd)))
    return lax.ppermute(value, PAIR, pairs)


def sources(pos_ref, near, far, color):
    dx, dy = (near, far) if color == 0 else (far, near)
    x = pos_ref[0] ^ (dx ^ (dx >> 1))
    y = pos_ref[1] ^ (dy ^ (dy >> 1))
    sign = 2 * (pos_ref[2] % 2) - 1
    start = (y // 2) * 32 + x
    return y % 2, [start + ((pos_ref[2] + sign * dz) & 7) * 4 for dz in Z_ORDER]


def phases(trans_list, count):
    half_width = BOX // 2 + 1
    freq_index = jnp.arange(count, dtype=jnp.int32)
    row_index = freq_index // half_width
    col_index = freq_index % half_width
    wave_x = (row_index - BOX * (row_index >= BOX // 2).astype(jnp.int32)).astype(jnp.float32)
    wave_y = col_index.astype(jnp.float32)
    shift_x = (trans_list % TGRID - TGRID // 2).astype(jnp.float32)
    shift_y = (trans_list // TGRID - TGRID // 2).astype(jnp.float32)
    angle = (
        2.0
        * math.pi
        / BOX
        * (shift_x[:, None] * wave_x[None, :] + shift_y[:, None] * wave_y[None, :])
    )
    return (jnp.cos(angle), jnp.sin(angle))


def iota(shape, dim):
    return lax.broadcasted_iota(jnp.int32, shape, dim)


def split3(value, axis=0):
    high = value.astype(jnp.bfloat16)
    rest = value - high.astype(jnp.float32)
    mid = rest.astype(jnp.bfloat16)
    low = (rest - mid.astype(jnp.float32)).astype(jnp.bfloat16)
    return jnp.concatenate([high, mid, low], axis=axis)


def mm(left, right, dims=((1,), (0,)), precision=None):
    return lax.dot_general(
        left, right, (dims, ((), ())), precision=precision, preferred_element_type=jnp.float32
    )


def pack_kernel(p_ref, a_ref, b_ref):
    lane = iota((8, LANE), 1)
    sub = iota((8, LANE), 0)
    for color, out in ((0, a_ref), (1, b_ref)):
        extra = jnp.zeros((8, LANE), jnp.float32)
        for kl in range(2):
            for c in range(2):
                rows = p_ref[0, color * 2 + kl, :, c, :].astype(jnp.float32)
                group = kl * 2 + c
                out[group * 8 : group * 8 + 8, :] = rows[:, :LANE].astype(jnp.bfloat16)
                first = 2 * (group * 8 + sub)
                extra += jnp.where(lane == first, rows[:, LANE : LANE + 1], 0.0)
                extra += jnp.where(lane == first + 1, rows[:, LANE + 1 : LANE + 2], 0.0)
        row = jnp.sum(extra, axis=0, keepdims=True)
        out[32:40, :] = jnp.broadcast_to(row, (8, LANE)).astype(jnp.bfloat16)


def pack_sections(projections):
    shape = jax.ShapeDtypeStruct((ROWS, LANE), jnp.bfloat16)
    return pl.pallas_call(pack_kernel, out_shape=(shape, shape), name="pack_sections")(projections)


def onehot_rows(group_row):
    onehot = (iota((G, NP), 0) == group_row).astype(jnp.float32)
    return jnp.concatenate([onehot, onehot, onehot], axis=0)


def weight_kernel(image_ref, table_ref, group_ref, out_ref, ctf_ref, onehot_ref):
    @pl.when(pl.program_id(0) == 0)
    def _():
        onehot_ref[...] = onehot_rows(group_ref[...]).T.astype(jnp.bfloat16)

    ctf_ref[...] = mm(onehot_ref[...], split3(table_ref[0]))

    def body(i, carry):
        rows = pl.ds(pl.multiple_of(i * 16, 16), 16)
        for c in range(2):
            value = image_ref[0, rows, c, :].astype(jnp.float32)
            value = (ctf_ref[rows, :] * value).astype(jnp.bfloat16)
            for tile in range(PART // LANE):
                start = (2 * tile + c) * LANE
                out_ref[rows, start : start + LANE] = value[:, tile * LANE : (tile + 1) * LANE]
        return carry

    lax.fori_loop(0, NP // 16, body, 0)


def weight_images(images, table, group_row):
    return pl.pallas_call(
        weight_kernel,
        grid=(FC // PART,),
        in_specs=[
            pl.BlockSpec((1, NP, 2, PART), lambda j: (0, 0, 0, j)),
            pl.BlockSpec((1, G, PART), lambda j: (0, 0, j)),
            pl.BlockSpec((1, NP), lambda j: (0, 0)),
        ],
        out_specs=pl.BlockSpec((NP, 2 * PART), lambda j: (0, j)),
        out_shape=jax.ShapeDtypeStruct((NP, 2 * FC), jnp.bfloat16),
        scratch_shapes=[
            pltpu.VMEM((NP, PART), jnp.float32),
            pltpu.VMEM((NP, 3 * G), jnp.bfloat16),
        ],
        compiler_params=pltpu.CompilerParams(vmem_limit_bytes=VMEM_LIMIT),
        name="weight_images",
    )(images, table, group_row)


def weight_copy(w_hbm, w_ref, sem_ref, step):
    lanes = pl.ds(pl.multiple_of(step * (2 * CHUNK), LANE), 2 * CHUNK)
    return pltpu.make_async_copy(w_hbm.at[:, lanes], w_ref.at[step], sem_ref.at[step])


def unpack_sections(pos_ref, a_refs, b_refs, nat_ref, ex_ref):
    lane = iota((32, LANE), 1)
    for color, refs in ((0, a_refs), (1, b_refs)):
        for near in range(4):
            ref = refs[near]

            def body(far, carry, ref=ref, near=near, color=color):
                cls, chunks = sources(pos_ref, near, far, color)
                rows = pl.ds(pl.multiple_of(cls * 64 + color * 32, 32), 32)
                for slot, j in enumerate(chunks):
                    piece = ref[far, slot].astype(jnp.float32)
                    turned = pltpu.roll(piece[:32], 2 * j, 1)
                    here = pl.ds(pl.multiple_of(j * LANE, LANE), LANE)
                    after = pl.ds(pl.multiple_of((j + 1) * LANE, LANE), LANE)
                    pltpu.store(nat_ref.at[rows, here], turned, mask=lane >= 2 * j)
                    pltpu.store(nat_ref.at[rows, after], turned, mask=lane < 2 * j)
                    ex_ref[pl.ds(cls * 128 + color * 64 + j, 1), :] = piece[32:33]
                return carry

            lax.fori_loop(0, 4, body, 0)
    for cls in range(2):
        for color in range(2):
            start = cls * 128 + color * 64
            extra = ex_ref[start : start + 64, :].astype(jnp.bfloat16)
            total = jnp.zeros((32, LANE), jnp.float32)
            for u in range(2):
                pick = (iota((32, LANE), 1) == 2 * iota((32, LANE), 0) + u).astype(jnp.float32)
                column = mm(pick.astype(jnp.bfloat16), extra, ((1,), (1,)))
                spread = (iota((64, LANE), 1) == 2 * iota((64, LANE), 0) + u).astype(jnp.float32)
                total += mm(column.astype(jnp.bfloat16), spread.astype(jnp.bfloat16))
            rows = slice(cls * 64 + color * 32, cls * 64 + color * 32 + 32)
            for t in range(1, TILES):
                here = slice(t * LANE, (t + 1) * LANE)
                pltpu.store(nat_ref.at[rows, here], total, mask=lane // 2 == t - 1)


def score_kernel(
    pos_ref, a0, a1, a2, a3, b0, b1, b2, b3, w_hbm, table_ref, inv_ref, cos_ref, sin_ref,
    group_ref, orient_ref, post_ref, left_ref, right_ref,
    nat_ref, ex_ref, shift_ref, acc_ref, norm_ref, w_ref, sem_ref,
):
    for step in range(STEPS):
        weight_copy(w_hbm, w_ref, sem_ref, step).start()
    unpack_sections(pos_ref, (a0, a1, a2, a3), (b0, b1, b2, b3), nat_ref, ex_ref)
    acc_ref[...] = jnp.zeros_like(acc_ref)
    norm_ref[...] = jnp.zeros_like(norm_ref)

    def shift(step, slot):
        for tile in range(CHUNK // LANE):
            here = pl.ds(pl.multiple_of(step * CHUNK + tile * LANE, LANE), LANE)
            inverse = jnp.broadcast_to(inv_ref[0:1, here], (8, LANE))
            cosine = jnp.broadcast_to(cos_ref[:, here][:, None, :], (TR, O, LANE))
            sine = jnp.broadcast_to(sin_ref[:, here][:, None, :], (TR, O, LANE))
            start = 2 * tile * LANE
            for k in range(K):
                real = (nat_ref[k * 16 : k * 16 + 8, here] * inverse)[None]
                imag = (nat_ref[k * 16 + 8 : k * 16 + 16, here] * inverse)[None]
                rows = slice(k * 64, k * 64 + 64)
                shift_ref[slot, rows, start : start + LANE] = (
                    (real * cosine - imag * sine).reshape(TR * O, LANE).astype(jnp.bfloat16)
                )
                shift_ref[slot, rows, start + LANE : start + 2 * LANE] = (
                    (real * sine + imag * cosine).reshape(TR * O, LANE).astype(jnp.bfloat16)
                )
        lanes = pl.ds(pl.multiple_of(step * CHUNK, LANE), CHUNK)
        table = table_ref[0, :, lanes]
        powers = []
        for k in range(K):
            real = nat_ref[k * 16 : k * 16 + 8, lanes]
            imag = nat_ref[k * 16 + 8 : k * 16 + 16, lanes]
            powers.append(real * real + imag * imag)
        power = jnp.concatenate(powers, axis=0)
        ctf_power = table * table * inv_ref[0:1, lanes]
        norm_ref[...] += mm(power, ctf_power, ((1,), (1,)), lax.Precision.HIGHEST)

    def multiply(step, slot):
        acc_ref[...] += mm(shift_ref[slot], w_ref[step], ((1,), (1,)))

    shift(0, 0)

    def body(j, carry):
        weight_copy(w_hbm, w_ref, sem_ref, 2 * j).wait()
        weight_copy(w_hbm, w_ref, sem_ref, 2 * j + 1).wait()
        shift(2 * j + 1, 1)
        multiply(2 * j, 0)
        shift(2 * j + 2, 0)
        multiply(2 * j + 1, 1)
        return carry

    lax.fori_loop(0, STEPS // 2, body, 0)
    weight_copy(w_hbm, w_ref, sem_ref, STEPS - 1).wait()
    multiply(STEPS - 1, 0)

    wide = K * TR * O
    row = iota((wide, K * O), 0)
    widen = (iota((wide, K * O), 1) == (row // (TR * O)) * O + row % O).astype(jnp.float32)
    norm_wide = mm(widen, norm_ref[...], precision=lax.Precision.HIGHEST)
    onehot3 = onehot_rows(group_ref[...]).astype(jnp.bfloat16)
    scores = acc_ref[...] - 0.5 * mm(split3(norm_wide, 1), onehot3)
    orient = iota((wide, NP), 0) % O
    mask = orient_ref[0:1, :] == orient
    for n in range(1, 4):
        mask = mask | (orient_ref[n : n + 1, :] == orient)
    top = jnp.max(jnp.where(mask, scores, -jnp.inf), axis=0, keepdims=True)
    expo = jnp.exp(jnp.where(mask, scores - top, -jnp.inf))
    total = jnp.sum(expo, axis=0, keepdims=True)
    live = (iota((1, NP), 1) < pos_ref[3]).astype(jnp.float32)
    weights = expo / total * live
    rounded = weights.astype(jnp.bfloat16)
    for cls in range(2):
        for color, out in ((0, left_ref), (1, right_ref)):
            k = cls * 4 + color * 2
            out[cls * 128 : cls * 128 + 128, :] = rounded[k * 64 : k * 64 + 128, :]
    row, col = iota((wide, wide), 0), iota((wide, wide), 1)
    target = (row // (TR * O)) * (TR * O) + (row % O) * TR + (row // O) % TR
    order = (col == target).astype(jnp.float32).astype(jnp.bfloat16)
    post_ref[0] = mm(weights.T.astype(jnp.bfloat16), order).astype(jnp.bfloat16)


SMEM = pl.BlockSpec(memory_space=pltpu.SMEM)
VMEM = pl.BlockSpec(memory_space=pltpu.VMEM)
ANY = pl.BlockSpec(memory_space=pl.ANY)


def score(pos, a, b, weighted, table, inverse, cosine, sine, group_row, orient):
    wide = K * O * TR
    return pl.pallas_call(
        score_kernel,
        in_specs=[SMEM] + [VMEM] * 8 + [ANY] + [VMEM] * 6,
        out_specs=[VMEM] * 3,
        scratch_shapes=[
            pltpu.VMEM((128, FC), jnp.float32),
            pltpu.VMEM((256, LANE), jnp.float32),
            pltpu.VMEM((2, wide, 2 * CHUNK), jnp.bfloat16),
            pltpu.VMEM((wide, NP), jnp.float32),
            pltpu.VMEM((K * O, G), jnp.float32),
            pltpu.VMEM((STEPS, NP, 2 * CHUNK), jnp.bfloat16),
            pltpu.SemaphoreType.DMA((STEPS,)),
        ],
        out_shape=[
            jax.ShapeDtypeStruct((1, NP, wide), jnp.bfloat16),
            jax.ShapeDtypeStruct((wide // 2, NP), jnp.bfloat16),
            jax.ShapeDtypeStruct((wide // 2, NP), jnp.bfloat16),
        ],
        compiler_params=pltpu.CompilerParams(vmem_limit_bytes=VMEM_LIMIT),
        name="score",
    )(pos, *a, *b, weighted, table, inverse, cosine, sine, group_row, orient)


def back_kernel(
    color, pos_ref, post_ref, w_hbm, cos_ref, sin_ref, p0, p1, p2, p3,
    slab_ref, sum_ref, ex_ref, w_ref, sem_ref,
):
    for step in range(STEPS):
        weight_copy(w_hbm, w_ref, sem_ref, step).start()

    def multiply(step, slot):
        sum_ref[slot] = mm(post_ref[...], w_ref[step])

    def combine(step, slot):
        for tile in range(CHUNK // LANE):
            here = pl.ds(pl.multiple_of(step * CHUNK + tile * LANE, LANE), LANE)
            cosine = jnp.broadcast_to(cos_ref[:, here][:, None, :], (TR, O, LANE))
            sine = jnp.broadcast_to(sin_ref[:, here][:, None, :], (TR, O, LANE))
            start = 2 * tile * LANE
            for k in range(4):
                rows = slice(k * 64, k * 64 + 64)
                real = sum_ref[slot, rows, start : start + LANE].reshape(TR, O, LANE)
                imag = sum_ref[slot, rows, start + LANE : start + 2 * LANE].reshape(TR, O, LANE)
                slab_ref[k * 16 : k * 16 + 8, here] = jnp.sum(
                    real * cosine + imag * sine, axis=0
                )
                slab_ref[k * 16 + 8 : k * 16 + 16, here] = jnp.sum(
                    imag * cosine - real * sine, axis=0
                )

    weight_copy(w_hbm, w_ref, sem_ref, 0).wait()
    multiply(0, 0)

    def body(j, carry):
        weight_copy(w_hbm, w_ref, sem_ref, 2 * j + 1).wait()
        weight_copy(w_hbm, w_ref, sem_ref, 2 * j + 2).wait()
        multiply(2 * j + 1, 1)
        combine(2 * j, 0)
        multiply(2 * j + 2, 0)
        combine(2 * j + 1, 1)
        return carry

    lax.fori_loop(0, STEPS // 2, body, 0)
    combine(STEPS - 1, 0)

    lane = iota((32, LANE), 1)
    for cls in range(2):
        rows = slice(cls * 32, cls * 32 + 32)
        tails = jnp.zeros((32, LANE), jnp.float32)
        for t in range(1, TILES):
            tails = jnp.where(lane // 2 == t - 1, slab_ref[rows, t * LANE : (t + 1) * LANE], tails)
        tails = tails.astype(jnp.bfloat16)
        total = jnp.zeros((64, LANE), jnp.float32)
        for u in range(2):
            pick = (iota((64, LANE), 1) == 2 * iota((64, LANE), 0) + u).astype(jnp.float32)
            column = mm(pick.astype(jnp.bfloat16), tails, ((1,), (1,)))
            spread = (iota((32, LANE), 1) == 2 * iota((32, LANE), 0) + u).astype(jnp.float32)
            total += mm(column.astype(jnp.bfloat16), spread.astype(jnp.bfloat16))
        ex_ref[cls * 64 : cls * 64 + 64, :] = total
    for near, out in enumerate((p0, p1, p2, p3)):

        def pack(far, carry, near=near, out=out):
            cls, chunks = sources(pos_ref, near, far, color)
            rows = pl.ds(pl.multiple_of(cls * 32, 32), 32)
            for slot, j in enumerate(chunks):
                here = pl.ds(pl.multiple_of(j * LANE, LANE), LANE)
                after = pl.ds(pl.multiple_of((j + 1) * LANE, LANE), LANE)
                both = jnp.where(lane >= 2 * j, slab_ref[rows, here], slab_ref[rows, after])
                main = pltpu.roll(both, LANE - 2 * j, 1)
                tail = ex_ref[pl.ds(cls * 64 + j, 1), :]
                out[far, slot, 0:32, :] = main.astype(jnp.bfloat16)
                out[far, slot, 32:40, :] = jnp.broadcast_to(tail, (8, LANE)).astype(jnp.bfloat16)
            return carry

        lax.fori_loop(0, 4, pack, 0)


def project_back(color, pos, post, weighted, cosine, sine):
    def kernel(*refs):
        back_kernel(color, *refs)

    return pl.pallas_call(
        kernel,
        in_specs=[SMEM, VMEM, ANY, VMEM, VMEM],
        out_specs=[VMEM] * 4,
        scratch_shapes=[
            pltpu.VMEM((64, FC), jnp.float32),
            pltpu.VMEM((2, NP, 2 * CHUNK), jnp.float32),
            pltpu.VMEM((128, LANE), jnp.float32),
            pltpu.VMEM((STEPS, NP, 2 * CHUNK), jnp.bfloat16),
            pltpu.SemaphoreType.DMA((STEPS,)),
        ],
        out_shape=[jax.ShapeDtypeStruct((4, NZ, ROWS, LANE), jnp.bfloat16)] * 4,
        compiler_params=pltpu.CompilerParams(vmem_limit_bytes=VMEM_LIMIT),
        name="project_back_" + str(color),
    )(pos, post, weighted, cosine, sine)


def finish_kernel(own_ref, partner_ref, slab_ref, product_ref):
    lane = iota((8, LANE), 1)
    sub = iota((8, LANE), 0)

    def tails(row, group):
        first = 2 * (group * 8 + sub)
        wide = jnp.broadcast_to(row, (8, LANE))
        one = jnp.sum(jnp.where(lane == first, wide, 0.0), axis=1, keepdims=True)
        two = jnp.sum(jnp.where(lane == first + 1, wide, 0.0), axis=1, keepdims=True)
        return jnp.concatenate([one, two], axis=1)

    for color in range(2):
        base = color * ROWS
        own_row = own_ref[base + 32 : base + 33, :]
        partner_row = partner_ref[base + 32 : base + 40, :].astype(jnp.float32)[0:1]
        for kl in range(2):
            k = color * 2 + kl
            main, edge = 0.0, 0.0
            for c in range(2):
                group = kl * 2 + c
                rows = slice(base + group * 8, base + group * 8 + 8)
                own = own_ref[rows, :]
                own_tail = tails(own_row, group)
                slab_ref[0, k, :, c, 0:LANE] = own
                slab_ref[0, k, :, c, LANE : LANE + 2] = own_tail
                main += own * partner_ref[rows, :].astype(jnp.float32)
                edge += own_tail * tails(partner_row, group)
            product_ref[0, k, :, 0:LANE] = main
            product_ref[0, k, :, LANE : LANE + 2] = edge


def finish(own, partner):
    return pl.pallas_call(
        finish_kernel,
        out_shape=(
            jax.ShapeDtypeStruct((1, 4, O, 2, 130), jnp.float32),
            jax.ShapeDtypeStruct((1, 4, O, 130), jnp.float32),
        ),
        name="finish",
    )(own, partner)


def added(parts):
    total = parts[0].astype(jnp.float32)
    for part in parts[1:]:
        total = total + part.astype(jnp.float32)
    return total


def on_device(images, projections, ctf_table, ctf_group, orient_ids, trans_ids, inv_sigma, counts):
    cls, img = lax.axis_index("cls"), lax.axis_index("img")
    pos = jnp.stack(
        [img % 4, 2 * (img // 32) + cls, (img // 4) % 8, counts[0, 0]]
    ).astype(jnp.int32)
    group_row = ctf_group

    left, right = pack_sections(projections)
    shard = jnp.concatenate([left, right], axis=0)
    along = shard[None]
    for odd in (-1, 1, -3):
        along = jnp.concatenate([along, trade_z(along, odd)])
    left, right = along[None, :, :ROWS], along[None, :, ROWS:]
    for mask in (1, 3):
        left = jnp.concatenate([left, trade(left, my=mask)])
        right = jnp.concatenate([right, trade(right, mx=mask)])
    lefts = [left] + [trade(left, mx=mask) for mask in GRAY[1:]]
    rights = [right] + [trade(right, my=mask) for mask in GRAY[1:]]

    cosine, sine = phases(trans_ids[0], FC)
    weighted = weight_images(images, ctf_table, group_row)
    posterior, post_left, post_right = score(
        pos, lefts, rights, weighted, ctf_table, inv_sigma, cosine, sine, group_row, orient_ids[0].T
    )

    pieces = project_back(0, pos, post_left, weighted, cosine, sine)
    left = added([pieces[0]] + [trade(pieces[d], mx=GRAY[d]) for d in range(1, 4)])
    pieces = project_back(1, pos, post_right, weighted, cosine, sine)
    right = added([pieces[0]] + [trade(pieces[d], my=GRAY[d]) for d in range(1, 4)])
    for mask, size in ((3, 2), (1, 1)):
        left, right = left.astype(jnp.bfloat16), right.astype(jnp.bfloat16)
        left = added([left[:size], trade(left[size:], my=mask)])
        right = added([right[:size], trade(right[size:], mx=mask)])
    own = jnp.concatenate([left[0], right[0]], axis=1)
    for odd, size in ((-3, 4), (1, 2), (-1, 1)):
        own = own.astype(jnp.bfloat16)
        own = added([own[:size], trade_z(own[size:], odd)])
    own = own[0]
    partner = lax.ppermute(own.astype(jnp.bfloat16), "half", [(0, 1), (1, 0)])
    slab, product = finish(own, partner)
    return (posterior, slab, product)


def solution(mesh):
    return jax.shard_map(
        on_device,
        mesh=mesh,
        in_specs=(
            P("half", ("cls", "img"), None, None),
            P("half", "cls", None, None, "img"),
            P("half", None, None),
            P("half", ("cls", "img")),
            P("half", ("cls", "img"), None),
            P("half", None),
            P("half", None),
            P("half", ("cls", "img")),
        ),
        out_specs=(
            P("half", ("cls", "img"), None),
            P("half", "cls", None, None, "img"),
            P("half", "cls", None, "img"),
        ),
        check_vma=False,
    )
```

```python
import math

import jax
import jax.numpy as jnp
from jax import lax
from jax.experimental import pallas as pl
from jax.experimental.pallas import tpu as pltpu
from jax.sharding import PartitionSpec as P


K = 8
BOX = 128
O = 8
TR = 8
TGRID = 5
FC = 8320
G = 32
NP = 256
LANE = 128
TILES = FC // LANE
CHUNK = 640
STEPS = FC // CHUNK
PARTS = (3, 3, 3, 4)
ROWS = 264
NX, NY, NZ = 4, 4, 8
GRAY = (0, 1, 3, 2)
Z_ORDER = (0, -1, 1, 2, -3, -2, -4, -5)
PAIR = ("cls", "img")
VMEM_LIMIT = 56 * 1024 * 1024


def place(index):
    cls, img = divmod(index, 64)
    y_hi, rest = divmod(img, 32)
    z, x = divmod(rest, 4)
    return x, 2 * y_hi + cls, z


def flat(x, y, z):
    x, y, z = x % NX, y % NY, z % NZ
    return (y % 2) * 64 + (y // 2) * 32 + z * 4 + x


def trade(value, mx=0, my=0):
    pairs = []
    for index in range(NX * NY * NZ):
        x, y, z = place(index)
        pairs.append((index, flat(x ^ mx, y ^ my, z)))
    return lax.ppermute(value, PAIR, pairs)


def trade_z(value, odd):
    pairs = []
    for index in range(NX * NY * NZ):
        x, y, z = place(index)
        pairs.append((index, flat(x, y, z + odd if z % 2 else z - odd)))
    return lax.ppermute(value, PAIR, pairs)


def sources(pos_ref, near, far, color):
    dx, dy = (near, far) if color == 0 else (far, near)
    x = pos_ref[0] ^ (dx ^ (dx >> 1))
    y = pos_ref[1] ^ (dy ^ (dy >> 1))
    sign = 2 * (pos_ref[2] % 2) - 1
    start = (y // 2) * 32 + x
    return y % 2, [start + ((pos_ref[2] + sign * dz) & 7) * 4 for dz in Z_ORDER]


def phases(trans_list, count):
    half_width = BOX // 2 + 1
    freq_index = jnp.arange(count, dtype=jnp.int32)
    row_index = freq_index // half_width
    col_index = freq_index % half_width
    wave_x = (row_index - BOX * (row_index >= BOX // 2).astype(jnp.int32)).astype(jnp.float32)
    wave_y = col_index.astype(jnp.float32)
    shift_x = (trans_list % TGRID - TGRID // 2).astype(jnp.float32)
    shift_y = (trans_list // TGRID - TGRID // 2).astype(jnp.float32)
    angle = (
        2.0
        * math.pi
        / BOX
        * (shift_x[:, None] * wave_x[None, :] + shift_y[:, None] * wave_y[None, :])
    )
    return (jnp.cos(angle), jnp.sin(angle))


def iota(shape, dim):
    return lax.broadcasted_iota(jnp.int32, shape, dim)


def split3(value, axis=0):
    high = value.astype(jnp.bfloat16)
    rest = value - high.astype(jnp.float32)
    mid = rest.astype(jnp.bfloat16)
    low = (rest - mid.astype(jnp.float32)).astype(jnp.bfloat16)
    return jnp.concatenate([high, mid, low], axis=axis)


def mm(left, right, dims=((1,), (0,)), precision=None):
    return lax.dot_general(
        left, right, (dims, ((), ())), precision=precision, preferred_element_type=jnp.float32
    )


def pack_kernel(p_ref, out_ref):
    lane = iota((8, LANE), 1)
    sub = iota((8, LANE), 0)
    tails = []
    for color in range(2):
        extra = jnp.zeros((8, LANE), jnp.float32)
        for kl in range(2):
            for c in range(2):
                rows = p_ref[0, color * 2 + kl, :, c, :].astype(jnp.float32)
                group = kl * 2 + c
                start = color * 32 + group * 8
                out_ref[start : start + 8, :] = rows[:, :LANE].astype(jnp.bfloat16)
                first = 2 * (group * 8 + sub)
                extra += jnp.where(lane == first, rows[:, LANE : LANE + 1], 0.0)
                extra += jnp.where(lane == first + 1, rows[:, LANE + 1 : LANE + 2], 0.0)
        tails.append(jnp.sum(extra, axis=0, keepdims=True))
    both = jnp.where(sub == 0, tails[0], tails[1])
    out_ref[64:72, :] = both.astype(jnp.bfloat16)


def pack_sections(projections):
    shape = jax.ShapeDtypeStruct((72, LANE), jnp.bfloat16)
    return pl.pallas_call(pack_kernel, out_shape=shape, name="pack_sections")(projections)


def onehot_rows(group_row):
    onehot = (iota((G, NP), 0) == group_row).astype(jnp.float32)
    return jnp.concatenate([onehot, onehot, onehot], axis=0)


def weight_kernel(image_ref, table_ref, group_ref, out_ref, ctf_ref, onehot_ref):
    @pl.when(pl.program_id(0) == 0)
    def _():
        onehot_ref[...] = onehot_rows(group_ref[...]).T.astype(jnp.bfloat16)

    ctf_ref[...] = mm(onehot_ref[...], split3(table_ref[0]))

    def body(i, carry):
        rows = pl.ds(pl.multiple_of(i * 16, 16), 16)
        for c in range(2):
            value = image_ref[0, rows, c, :].astype(jnp.float32)
            value = (ctf_ref[rows, :] * value).astype(jnp.bfloat16)
            for tile in range(CHUNK // LANE):
                start = (2 * tile + c) * LANE
                out_ref[rows, start : start + LANE] = value[:, tile * LANE : (tile + 1) * LANE]
        return carry

    lax.fori_loop(0, NP // 16, body, 0)


def weight_images(part, images, table, group_row):
    first, count = sum(PARTS[:part]), PARTS[part]
    return pl.pallas_call(
        weight_kernel,
        grid=(count,),
        in_specs=[
            pl.BlockSpec((1, NP, 2, CHUNK), lambda j: (0, 0, 0, first + j)),
            pl.BlockSpec((1, G, CHUNK), lambda j: (0, 0, first + j)),
            pl.BlockSpec((1, NP), lambda j: (0, 0)),
        ],
        out_specs=pl.BlockSpec((NP, 2 * CHUNK), lambda j: (0, j)),
        out_shape=jax.ShapeDtypeStruct((NP, 2 * CHUNK * count), jnp.bfloat16),
        scratch_shapes=[
            pltpu.VMEM((NP, CHUNK), jnp.float32),
            pltpu.VMEM((NP, 3 * G), jnp.bfloat16),
        ],
        compiler_params=pltpu.CompilerParams(vmem_limit_bytes=VMEM_LIMIT),
    )(images, table, group_row)


def start_copies(w_hbms, w_ref, sem_ref):
    step = 0
    for part, count in enumerate(PARTS):
        for n in range(count):
            lanes = slice(n * 2 * CHUNK, (n + 1) * 2 * CHUNK)
            pltpu.make_async_copy(w_hbms[part].at[:, lanes], w_ref.at[step], sem_ref.at[step]).start()
            step += 1


def wait_copy(w_hbms, w_ref, sem_ref, step):
    source = w_hbms[0].at[:, 0 : 2 * CHUNK]
    pltpu.make_async_copy(source, w_ref.at[step], sem_ref.at[step]).wait()


def unpack_sections(pos_ref, a_refs, b_refs, nat_ref, ex_ref):
    lane = iota((32, LANE), 1)
    for color, refs in ((0, a_refs), (1, b_refs)):
        for near in range(4):
            ref = refs[near]

            def body(far, carry, ref=ref, near=near, color=color):
                cls, chunks = sources(pos_ref, near, far, color)
                rows = pl.ds(pl.multiple_of(cls * 64 + color * 32, 32), 32)
                tails = ref[far, 256:264].astype(jnp.float32)
                for slot, j in enumerate(chunks):
                    piece = ref[far, slot * 32 : slot * 32 + 32].astype(jnp.float32)
                    turned = pltpu.roll(piece, 2 * j, 1)
                    here = pl.ds(pl.multiple_of(j * LANE, LANE), LANE)
                    after = pl.ds(pl.multiple_of((j + 1) * LANE, LANE), LANE)
                    pltpu.store(nat_ref.at[rows, here], turned, mask=lane >= 2 * j)
                    pltpu.store(nat_ref.at[rows, after], turned, mask=lane < 2 * j)
                    ex_ref[pl.ds(cls * 128 + color * 64 + j, 1), :] = tails[slot : slot + 1]
                return carry

            lax.fori_loop(0, 4, body, 0)
    for cls in range(2):
        for color in range(2):
            start = cls * 128 + color * 64
            extra = ex_ref[start : start + 64, :].astype(jnp.bfloat16)
            total = jnp.zeros((32, LANE), jnp.float32)
            for u in range(2):
                pick = (iota((32, LANE), 1) == 2 * iota((32, LANE), 0) + u).astype(jnp.float32)
                column = mm(pick.astype(jnp.bfloat16), extra, ((1,), (1,)))
                spread = (iota((64, LANE), 1) == 2 * iota((64, LANE), 0) + u).astype(jnp.float32)
                total += mm(column.astype(jnp.bfloat16), spread.astype(jnp.bfloat16))
            rows = slice(cls * 64 + color * 32, cls * 64 + color * 32 + 32)
            for t in range(1, TILES):
                here = slice(t * LANE, (t + 1) * LANE)
                pltpu.store(nat_ref.at[rows, here], total, mask=lane // 2 == t - 1)


def score_kernel(
    pos_ref, a0, a1, a2, a3, b0, b1, b2, b3, w0, w1, w2, w3, table_ref, inv_ref,
    cos_ref, sin_ref, group_ref, orient_ref, left_ref, right_ref,
    nat_ref, ex_ref, shift_ref, acc_ref, norm_ref, w_ref, sem_ref,
):
    w_hbms = (w0, w1, w2, w3)
    start_copies(w_hbms, w_ref, sem_ref)
    unpack_sections(pos_ref, (a0, a1, a2, a3), (b0, b1, b2, b3), nat_ref, ex_ref)
    acc_ref[...] = jnp.zeros_like(acc_ref)
    norm_ref[...] = jnp.zeros_like(norm_ref)

    def shift(step, slot):
        for tile in range(CHUNK // LANE):
            here = pl.ds(pl.multiple_of(step * CHUNK + tile * LANE, LANE), LANE)
            inverse = jnp.broadcast_to(inv_ref[0:1, here], (8, LANE))
            cosine = jnp.broadcast_to(cos_ref[:, here][:, None, :], (TR, O, LANE))
            sine = jnp.broadcast_to(sin_ref[:, here][:, None, :], (TR, O, LANE))
            start = 2 * tile * LANE
            for k in range(K):
                real = (nat_ref[k * 16 : k * 16 + 8, here] * inverse)[None]
                imag = (nat_ref[k * 16 + 8 : k * 16 + 16, here] * inverse)[None]
                rows = slice(k * 64, k * 64 + 64)
                shift_ref[slot, rows, start : start + LANE] = (
                    (real * cosine - imag * sine).reshape(TR * O, LANE).astype(jnp.bfloat16)
                )
                shift_ref[slot, rows, start + LANE : start + 2 * LANE] = (
                    (real * sine + imag * cosine).reshape(TR * O, LANE).astype(jnp.bfloat16)
                )
        lanes = pl.ds(pl.multiple_of(step * CHUNK, LANE), CHUNK)
        table = table_ref[0, :, lanes]
        powers = []
        for k in range(K):
            real = nat_ref[k * 16 : k * 16 + 8, lanes]
            imag = nat_ref[k * 16 + 8 : k * 16 + 16, lanes]
            powers.append(real * real + imag * imag)
        power = jnp.concatenate(powers, axis=0)
        ctf_power = table * table * inv_ref[0:1, lanes]
        norm_ref[...] += mm(power, ctf_power, ((1,), (1,)), lax.Precision.HIGHEST)

    def multiply(step, slot):
        acc_ref[...] += mm(shift_ref[slot], w_ref[step], ((1,), (1,)))

    shift(0, 0)

    def body(j, carry):
        wait_copy(w_hbms, w_ref, sem_ref, 2 * j)
        wait_copy(w_hbms, w_ref, sem_ref, 2 * j + 1)
        shift(2 * j + 1, 1)
        multiply(2 * j, 0)
        shift(2 * j + 2, 0)
        multiply(2 * j + 1, 1)
        return carry

    lax.fori_loop(0, STEPS // 2, body, 0)
    wait_copy(w_hbms, w_ref, sem_ref, STEPS - 1)
    multiply(STEPS - 1, 0)

    wide = K * TR * O
    row = iota((wide, K * O), 0)
    widen = (iota((wide, K * O), 1) == (row // (TR * O)) * O + row % O).astype(jnp.float32)
    norm_wide = mm(widen, norm_ref[...], precision=lax.Precision.HIGHEST)
    onehot3 = onehot_rows(group_ref[...]).astype(jnp.bfloat16)
    scores = acc_ref[...] - 0.5 * mm(split3(norm_wide, 1), onehot3)
    orient = iota((wide, NP), 0) % O
    mask = orient_ref[0:1, :] == orient
    for n in range(1, 4):
        mask = mask | (orient_ref[n : n + 1, :] == orient)
    top = jnp.max(jnp.where(mask, scores, -jnp.inf), axis=0, keepdims=True)
    expo = jnp.exp(jnp.where(mask, scores - top, -jnp.inf))
    total = jnp.sum(expo, axis=0, keepdims=True)
    live = (iota((1, NP), 1) < pos_ref[3]).astype(jnp.float32)
    weights = expo / total * live
    rounded = weights.astype(jnp.bfloat16)
    for cls in range(2):
        for color, out in ((0, left_ref), (1, right_ref)):
            k = cls * 4 + color * 2
            out[cls * 128 : cls * 128 + 128, :] = rounded[k * 64 : k * 64 + 128, :]


def order_kernel(left_ref, right_ref, post_ref):
    wide = K * TR * O
    row, col = iota((wide, wide), 0), iota((wide, wide), 1)
    target = (row // (TR * O)) * (TR * O) + (row % O) * TR + (row // O) % TR
    order = (col == target).astype(jnp.float32).astype(jnp.bfloat16)
    rows = []
    for cls in range(2):
        for ref in (left_ref, right_ref):
            rows.append(ref[cls * 128 : cls * 128 + 128, :].astype(jnp.float32))
    turned = jnp.concatenate(rows, axis=0).T.astype(jnp.bfloat16)
    post_ref[0] = mm(turned, order).astype(jnp.bfloat16)


def order_posterior(left, right):
    return pl.pallas_call(
        order_kernel,
        out_shape=jax.ShapeDtypeStruct((1, NP, K * TR * O), jnp.bfloat16),
        name="order_posterior",
    )(left, right)


SMEM = pl.BlockSpec(memory_space=pltpu.SMEM)
VMEM = pl.BlockSpec(memory_space=pltpu.VMEM)
ANY = pl.BlockSpec(memory_space=pl.ANY)


def score(pos, a, b, weighted, table, inverse, cosine, sine, group_row, orient):
    wide = K * O * TR
    return pl.pallas_call(
        score_kernel,
        in_specs=[SMEM] + [VMEM] * 8 + [ANY] * 4 + [VMEM] * 6,
        out_specs=[VMEM] * 2,
        scratch_shapes=[
            pltpu.VMEM((128, FC), jnp.float32),
            pltpu.VMEM((256, LANE), jnp.float32),
            pltpu.VMEM((2, wide, 2 * CHUNK), jnp.bfloat16),
            pltpu.VMEM((wide, NP), jnp.float32),
            pltpu.VMEM((K * O, G), jnp.float32),
            pltpu.VMEM((STEPS, NP, 2 * CHUNK), jnp.bfloat16),
            pltpu.SemaphoreType.DMA((STEPS,)),
        ],
        out_shape=[
            jax.ShapeDtypeStruct((wide // 2, NP), jnp.bfloat16),
            jax.ShapeDtypeStruct((wide // 2, NP), jnp.bfloat16),
        ],
        compiler_params=pltpu.CompilerParams(vmem_limit_bytes=VMEM_LIMIT),
        name="score",
    )(pos, *a, *b, *weighted, table, inverse, cosine, sine, group_row, orient)


def back_kernel(
    color, pos_ref, post_ref, w0, w1, w2, w3, cos_ref, sin_ref, p0, p1, p2, p3,
    slab_ref, sum_ref, ex_ref, w_ref, sem_ref,
):
    w_hbms = (w0, w1, w2, w3)
    start_copies(w_hbms, w_ref, sem_ref)

    def multiply(step, slot):
        sum_ref[slot] = mm(post_ref[...], w_ref[step])

    def combine(step, slot):
        for tile in range(CHUNK // LANE):
            here = pl.ds(pl.multiple_of(step * CHUNK + tile * LANE, LANE), LANE)
            cosine = jnp.broadcast_to(cos_ref[:, here][:, None, :], (TR, O, LANE))
            sine = jnp.broadcast_to(sin_ref[:, here][:, None, :], (TR, O, LANE))
            start = 2 * tile * LANE
            for k in range(4):
                rows = slice(k * 64, k * 64 + 64)
                real = sum_ref[slot, rows, start : start + LANE].reshape(TR, O, LANE)
                imag = sum_ref[slot, rows, start + LANE : start + 2 * LANE].reshape(TR, O, LANE)
                slab_ref[k * 16 : k * 16 + 8, here] = jnp.sum(
                    real * cosine + imag * sine, axis=0
                )
                slab_ref[k * 16 + 8 : k * 16 + 16, here] = jnp.sum(
                    imag * cosine - real * sine, axis=0
                )

    wait_copy(w_hbms, w_ref, sem_ref, 0)
    multiply(0, 0)

    def body(j, carry):
        wait_copy(w_hbms, w_ref, sem_ref, 2 * j + 1)
        wait_copy(w_hbms, w_ref, sem_ref, 2 * j + 2)
        multiply(2 * j + 1, 1)
        combine(2 * j, 0)
        multiply(2 * j + 2, 0)
        combine(2 * j + 1, 1)
        return carry

    lax.fori_loop(0, STEPS // 2, body, 0)
    combine(STEPS - 1, 0)

    lane = iota((32, LANE), 1)
    for cls in range(2):
        rows = slice(cls * 32, cls * 32 + 32)
        tails = jnp.zeros((32, LANE), jnp.float32)
        for t in range(1, TILES):
            tails = jnp.where(lane // 2 == t - 1, slab_ref[rows, t * LANE : (t + 1) * LANE], tails)
        tails = tails.astype(jnp.bfloat16)
        total = jnp.zeros((64, LANE), jnp.float32)
        for u in range(2):
            pick = (iota((64, LANE), 1) == 2 * iota((64, LANE), 0) + u).astype(jnp.float32)
            column = mm(pick.astype(jnp.bfloat16), tails, ((1,), (1,)))
            spread = (iota((32, LANE), 1) == 2 * iota((32, LANE), 0) + u).astype(jnp.float32)
            total += mm(column.astype(jnp.bfloat16), spread.astype(jnp.bfloat16))
        ex_ref[cls * 64 : cls * 64 + 64, :] = total
    for near, out in enumerate((p0, p1, p2, p3)):

        def pack(far, carry, near=near, out=out):
            cls, chunks = sources(pos_ref, near, far, color)
            rows = pl.ds(pl.multiple_of(cls * 32, 32), 32)
            tails = []
            for slot, j in enumerate(chunks):
                here = pl.ds(pl.multiple_of(j * LANE, LANE), LANE)
                after = pl.ds(pl.multiple_of((j + 1) * LANE, LANE), LANE)
                both = jnp.where(lane >= 2 * j, slab_ref[rows, here], slab_ref[rows, after])
                main = pltpu.roll(both, LANE - 2 * j, 1)
                tails.append(ex_ref[pl.ds(cls * 64 + j, 1), :])
                out[far, slot * 32 : slot * 32 + 32, :] = main.astype(jnp.bfloat16)
            out[far, 256:264, :] = jnp.concatenate(tails, axis=0).astype(jnp.bfloat16)
            return carry

        lax.fori_loop(0, 4, pack, 0)


def project_back(color, pos, post, weighted, cosine, sine):
    def kernel(*refs):
        back_kernel(color, *refs)

    return pl.pallas_call(
        kernel,
        in_specs=[SMEM, VMEM] + [ANY] * 4 + [VMEM] * 2,
        out_specs=[VMEM] * 4,
        scratch_shapes=[
            pltpu.VMEM((64, FC), jnp.float32),
            pltpu.VMEM((2, NP, 2 * CHUNK), jnp.float32),
            pltpu.VMEM((128, LANE), jnp.float32),
            pltpu.VMEM((STEPS, NP, 2 * CHUNK), jnp.bfloat16),
            pltpu.SemaphoreType.DMA((STEPS,)),
        ],
        out_shape=[jax.ShapeDtypeStruct((4, ROWS, LANE), jnp.bfloat16)] * 4,
        compiler_params=pltpu.CompilerParams(vmem_limit_bytes=VMEM_LIMIT),
    )(pos, post, *weighted, cosine, sine)


def finish_kernel(own_ref, partner_ref, slab_ref, product_ref):
    lane = iota((8, LANE), 1)
    sub = iota((8, LANE), 0)

    def tails(row, group):
        first = 2 * (group * 8 + sub)
        wide = jnp.broadcast_to(row, (8, LANE))
        one = jnp.sum(jnp.where(lane == first, wide, 0.0), axis=1, keepdims=True)
        two = jnp.sum(jnp.where(lane == first + 1, wide, 0.0), axis=1, keepdims=True)
        return jnp.concatenate([one, two], axis=1)

    for color in range(2):
        base = color * 32
        own_row = own_ref[64 + color : 65 + color, :]
        partner_row = partner_ref[64:72, :].astype(jnp.float32)[color : color + 1]
        for kl in range(2):
            k = color * 2 + kl
            main, edge = 0.0, 0.0
            for c in range(2):
                group = kl * 2 + c
                rows = slice(base + group * 8, base + group * 8 + 8)
                own = own_ref[rows, :]
                own_tail = tails(own_row, group)
                slab_ref[0, k, :, c, 0:LANE] = own
                slab_ref[0, k, :, c, LANE : LANE + 2] = own_tail
                main += own * partner_ref[rows, :].astype(jnp.float32)
                edge += own_tail * tails(partner_row, group)
            product_ref[0, k, :, 0:LANE] = main
            product_ref[0, k, :, LANE : LANE + 2] = edge


def finish(own, partner):
    return pl.pallas_call(
        finish_kernel,
        out_shape=(
            jax.ShapeDtypeStruct((1, 4, O, 2, 130), jnp.float32),
            jax.ShapeDtypeStruct((1, 4, O, 130), jnp.float32),
        ),
        name="finish",
    )(own, partner)


def regroup_kernel(own_ref, got_ref, left_ref, right_ref):
    tails = ([], [])
    for slot in range(NZ):
        ref = own_ref if slot < 4 else got_ref
        last = ref[slot % 4, 64:72, :].astype(jnp.float32)
        for color, out in ((0, left_ref), (1, right_ref)):
            out[0, slot * 32 : slot * 32 + 32, :] = ref[slot % 4, color * 32 : color * 32 + 32, :]
            tails[color].append(last[color : color + 1])
    left_ref[0, 256:264, :] = jnp.concatenate(tails[0], axis=0).astype(jnp.bfloat16)
    right_ref[0, 256:264, :] = jnp.concatenate(tails[1], axis=0).astype(jnp.bfloat16)


def regroup(own, got):
    shape = jax.ShapeDtypeStruct((1, ROWS, LANE), jnp.bfloat16)
    return pl.pallas_call(regroup_kernel, out_shape=(shape, shape), name="regroup")(own, got)


def ungroup_kernel(l0_ref, l1_ref, r0_ref, r1_ref, keep_ref, send_ref):
    sub = iota((8, LANE), 0)
    tails = []
    for first, second in ((l0_ref, l1_ref), (r0_ref, r1_ref)):
        tails.append(first[0, 256:264, :] + second[0, 256:264, :].astype(jnp.float32))
    for slot in range(NZ):
        parts = []
        rows = slice(slot * 32, slot * 32 + 32)
        for first, second in ((l0_ref, l1_ref), (r0_ref, r1_ref)):
            parts.append(first[0, rows, :] + second[0, rows, :].astype(jnp.float32))
        left, right = tails[0][slot : slot + 1], tails[1][slot : slot + 1]
        parts.append(jnp.where(sub == 0, left, jnp.where(sub == 1, right, 0.0)))
        value = jnp.concatenate(parts, axis=0)
        if slot < 4:
            keep_ref[slot] = value
        else:
            send_ref[slot - 4] = value.astype(jnp.bfloat16)


def ungroup(l0, l1, r0, r1):
    return pl.pallas_call(
        ungroup_kernel,
        out_shape=(
            jax.ShapeDtypeStruct((4, 72, LANE), jnp.float32),
            jax.ShapeDtypeStruct((4, 72, LANE), jnp.bfloat16),
        ),
        name="ungroup",
    )(l0, l1, r0, r1)


def added(parts):
    total = parts[0].astype(jnp.float32)
    for part in parts[1:]:
        total = total + part.astype(jnp.float32)
    return total


def run(images, projections, ctf_table, ctf_group, orient_ids, trans_ids, inv_sigma, counts):
    cls, img = lax.axis_index("cls"), lax.axis_index("img")
    pos = jnp.stack(
        [img % 4, 2 * (img // 32) + cls, (img // 4) % 8, counts[0, 0]]
    ).astype(jnp.int32)
    cosine, sine = phases(trans_ids[0], FC)
    weighted = []
    for part in range(len(PARTS)):
        weighted.append(weight_images(part, images, ctf_table, ctf_group))

    along = pack_sections(projections)[None]
    for odd in (-1, 1):
        along = jnp.concatenate([along, trade_z(along, odd)])
    got = trade_z(along, -3)
    left, right = regroup(along, got)
    for mask in (1, 3):
        left = jnp.concatenate([left, trade(left, my=mask)])
        right = jnp.concatenate([right, trade(right, mx=mask)])
    lefts, rights = [left], [right]
    for mask in GRAY[1:]:
        lefts.append(trade(left, mx=mask))
    for mask in GRAY[1:]:
        rights.append(trade(right, my=mask))

    post_left, post_right = score(
        pos, lefts, rights, weighted, ctf_table, inv_sigma, cosine, sine, ctf_group, orient_ids[0].T
    )

    pieces = project_back(0, pos, post_left, weighted, cosine, sine)
    left = added([pieces[0]] + [trade(pieces[d], mx=GRAY[d]) for d in range(1, 4)])
    pieces = project_back(1, pos, post_right, weighted, cosine, sine)
    parts = [pieces[0]]
    for d in range(1, 4):
        parts.append(trade(pieces[d], my=GRAY[d]))
    right = added(parts)
    posterior = order_posterior(post_left, post_right)
    left = added([left[:2], trade(left[2:].astype(jnp.bfloat16), my=3)])
    right = added([right[:2], trade(right[2:].astype(jnp.bfloat16), mx=3)])
    left_got = trade(left[1:].astype(jnp.bfloat16), my=1)
    right_got = trade(right[1:].astype(jnp.bfloat16), mx=1)
    own, sent = ungroup(left[:1], left_got, right[:1], right_got)
    own = own + trade_z(sent, -3).astype(jnp.float32)
    for odd, size in ((1, 2), (-1, 1)):
        own = added([own[:size], trade_z(own[size:].astype(jnp.bfloat16), odd)])
    own = own[0]
    partner = lax.ppermute(own.astype(jnp.bfloat16), "half", [(0, 1), (1, 0)])
    slab, product = finish(own, partner)
    return (posterior, slab, product)


def solution(mesh):
    return jax.shard_map(
        run,
        mesh=mesh,
        in_specs=(
            P("half", ("cls", "img"), None, None),
            P("half", "cls", None, None, "img"),
            P("half", None, None),
            P("half", ("cls", "img")),
            P("half", ("cls", "img"), None),
            P("half", None),
            P("half", None),
            P("half", ("cls", "img")),
        ),
        out_specs=(
            P("half", ("cls", "img"), None),
            P("half", "cls", None, None, "img"),
            P("half", "cls", None, "img"),
        ),
        check_vma=False,
    )
```

```python
import math

import jax
import jax.numpy as jnp
from jax import lax
from jax.experimental import pallas as pl
from jax.experimental.pallas import tpu as pltpu
from jax.sharding import PartitionSpec as P


K = 8
BOX = 128
O = 8
TR = 8
TGRID = 5
FC = 8320
G = 32
NP = 256
LANE = 128
TILES = FC // LANE
CHUNK = 640
STEPS = FC // CHUNK
PART = 1664
ROWS = 264
NX, NY, NZ = 4, 4, 8
GRAY = (0, 1, 3, 2)
Z_ORDER = (0, -1, 1, 2, -3, -2, -4, -5)
PAIR = ("cls", "img")
VMEM_LIMIT = 56 * 1024 * 1024


def place(index):
    cls, img = divmod(index, 64)
    y_hi, rest = divmod(img, 32)
    z, x = divmod(rest, 4)
    return x, 2 * y_hi + cls, z


def flat(x, y, z):
    x, y, z = x % NX, y % NY, z % NZ
    return (y % 2) * 64 + (y // 2) * 32 + z * 4 + x


def trade(value, mx=0, my=0):
    pairs = []
    for index in range(NX * NY * NZ):
        x, y, z = place(index)
        pairs.append((index, flat(x ^ mx, y ^ my, z)))
    return lax.ppermute(value, PAIR, pairs)


def trade_z(value, odd):
    pairs = []
    for index in range(NX * NY * NZ):
        x, y, z = place(index)
        pairs.append((index, flat(x, y, z + odd if z % 2 else z - odd)))
    return lax.ppermute(value, PAIR, pairs)


def sources(pos_ref, near, far, color):
    dx, dy = (near, far) if color == 0 else (far, near)
    x = pos_ref[0] ^ (dx ^ (dx >> 1))
    y = pos_ref[1] ^ (dy ^ (dy >> 1))
    sign = 2 * (pos_ref[2] % 2) - 1
    start = (y // 2) * 32 + x
    return y % 2, [start + ((pos_ref[2] + sign * dz) & 7) * 4 for dz in Z_ORDER]


def phases(trans_list, count):
    half_width = BOX // 2 + 1
    freq_index = jnp.arange(count, dtype=jnp.int32)
    row_index = freq_index // half_width
    col_index = freq_index % half_width
    wave_x = (row_index - BOX * (row_index >= BOX // 2).astype(jnp.int32)).astype(jnp.float32)
    wave_y = col_index.astype(jnp.float32)
    shift_x = (trans_list % TGRID - TGRID // 2).astype(jnp.float32)
    shift_y = (trans_list // TGRID - TGRID // 2).astype(jnp.float32)
    angle = (
        2.0
        * math.pi
        / BOX
        * (shift_x[:, None] * wave_x[None, :] + shift_y[:, None] * wave_y[None, :])
    )
    return (jnp.cos(angle), jnp.sin(angle))


def iota(shape, dim):
    return lax.broadcasted_iota(jnp.int32, shape, dim)


def split3(value, axis=0):
    high = value.astype(jnp.bfloat16)
    rest = value - high.astype(jnp.float32)
    mid = rest.astype(jnp.bfloat16)
    low = (rest - mid.astype(jnp.float32)).astype(jnp.bfloat16)
    return jnp.concatenate([high, mid, low], axis=axis)


def mm(left, right, dims=((1,), (0,)), precision=None):
    return lax.dot_general(
        left, right, (dims, ((), ())), precision=precision, preferred_element_type=jnp.float32
    )


def pack_kernel(p_ref, out_ref):
    lane = iota((8, LANE), 1)
    sub = iota((8, LANE), 0)
    tails = []
    for color in range(2):
        extra = jnp.zeros((8, LANE), jnp.float32)
        for kl in range(2):
            for c in range(2):
                rows = p_ref[0, color * 2 + kl, :, c, :].astype(jnp.float32)
                group = kl * 2 + c
                start = color * 32 + group * 8
                out_ref[start : start + 8, :] = rows[:, :LANE].astype(jnp.bfloat16)
                first = 2 * (group * 8 + sub)
                extra += jnp.where(lane == first, rows[:, LANE : LANE + 1], 0.0)
                extra += jnp.where(lane == first + 1, rows[:, LANE + 1 : LANE + 2], 0.0)
        tails.append(jnp.sum(extra, axis=0, keepdims=True))
    both = jnp.where(sub == 0, tails[0], tails[1])
    out_ref[64:72, :] = both.astype(jnp.bfloat16)


def pack_sections(projections):
    shape = jax.ShapeDtypeStruct((72, LANE), jnp.bfloat16)
    return pl.pallas_call(pack_kernel, out_shape=shape, name="pack_sections")(projections)


def onehot_rows(group_row):
    onehot = (iota((G, NP), 0) == group_row).astype(jnp.float32)
    return jnp.concatenate([onehot, onehot, onehot], axis=0)


def weight_kernel(image_ref, table_ref, group_ref, out_ref, ctf_ref, onehot_ref):
    @pl.when(pl.program_id(0) == 0)
    def _():
        onehot_ref[...] = onehot_rows(group_ref[...]).T.astype(jnp.bfloat16)

    ctf_ref[...] = mm(onehot_ref[...], split3(table_ref[0]))

    def body(i, carry):
        rows = pl.ds(pl.multiple_of(i * 16, 16), 16)
        for c in range(2):
            value = image_ref[0, rows, c, :].astype(jnp.float32)
            value = (ctf_ref[rows, :] * value).astype(jnp.bfloat16)
            for tile in range(PART // LANE):
                start = (2 * tile + c) * LANE
                out_ref[rows, start : start + LANE] = value[:, tile * LANE : (tile + 1) * LANE]
        return carry

    lax.fori_loop(0, NP // 16, body, 0)


def weight_images(images, table, group_row):
    return pl.pallas_call(
        weight_kernel,
        grid=(FC // PART,),
        in_specs=[
            pl.BlockSpec((1, NP, 2, PART), lambda j: (0, 0, 0, j)),
            pl.BlockSpec((1, G, PART), lambda j: (0, 0, j)),
            pl.BlockSpec((1, NP), lambda j: (0, 0)),
        ],
        out_specs=pl.BlockSpec((NP, 2 * PART), lambda j: (0, j)),
        out_shape=jax.ShapeDtypeStruct((NP, 2 * FC), jnp.bfloat16),
        scratch_shapes=[
            pltpu.VMEM((NP, PART), jnp.float32),
            pltpu.VMEM((NP, 3 * G), jnp.bfloat16),
        ],
        compiler_params=pltpu.CompilerParams(vmem_limit_bytes=VMEM_LIMIT),
        name="weight_images",
    )(images, table, group_row)


def weight_copy(w_hbm, w_ref, sem_ref, step):
    lanes = pl.ds(pl.multiple_of(step * (2 * CHUNK), LANE), 2 * CHUNK)
    return pltpu.make_async_copy(w_hbm.at[:, lanes], w_ref.at[step], sem_ref.at[step])


def unpack_sections(pos_ref, a_refs, b_refs, nat_ref, ex_ref):
    lane = iota((32, LANE), 1)
    for color, refs in ((0, a_refs), (1, b_refs)):
        for near in range(4):
            ref = refs[near]

            def body(far, carry, ref=ref, near=near, color=color):
                cls, chunks = sources(pos_ref, near, far, color)
                rows = pl.ds(pl.multiple_of(cls * 64 + color * 32, 32), 32)
                tails = ref[far, 256:264].astype(jnp.float32)
                for slot, j in enumerate(chunks):
                    piece = ref[far, slot * 32 : slot * 32 + 32].astype(jnp.float32)
                    turned = pltpu.roll(piece, 2 * j, 1)
                    here = pl.ds(pl.multiple_of(j * LANE, LANE), LANE)
                    after = pl.ds(pl.multiple_of((j + 1) * LANE, LANE), LANE)
                    pltpu.store(nat_ref.at[rows, here], turned, mask=lane >= 2 * j)
                    pltpu.store(nat_ref.at[rows, after], turned, mask=lane < 2 * j)
                    ex_ref[pl.ds(cls * 128 + color * 64 + j, 1), :] = tails[slot : slot + 1]
                return carry

            lax.fori_loop(0, 4, body, 0)
    for cls in range(2):
        for color in range(2):
            start = cls * 128 + color * 64
            extra = ex_ref[start : start + 64, :].astype(jnp.bfloat16)
            total = jnp.zeros((32, LANE), jnp.float32)
            for u in range(2):
                pick = (iota((32, LANE), 1) == 2 * iota((32, LANE), 0) + u).astype(jnp.float32)
                column = mm(pick.astype(jnp.bfloat16), extra, ((1,), (1,)))
                spread = (iota((64, LANE), 1) == 2 * iota((64, LANE), 0) + u).astype(jnp.float32)
                total += mm(column.astype(jnp.bfloat16), spread.astype(jnp.bfloat16))
            rows = slice(cls * 64 + color * 32, cls * 64 + color * 32 + 32)
            for t in range(1, TILES):
                here = slice(t * LANE, (t + 1) * LANE)
                pltpu.store(nat_ref.at[rows, here], total, mask=lane // 2 == t - 1)


def score_kernel(
    pos_ref, a0, a1, a2, a3, b0, b1, b2, b3, w_hbm, table_ref, inv_ref,
    cos_ref, sin_ref, group_ref, orient_ref, left_ref, right_ref, p0, p1, p2, p3,
    nat_ref, ex_ref, shift_ref, acc_ref, norm_ref, w_ref, sem_ref, slab_ref, sum_ref,
):
    for step in range(STEPS):
        weight_copy(w_hbm, w_ref, sem_ref, step).start()
    unpack_sections(pos_ref, (a0, a1, a2, a3), (b0, b1, b2, b3), nat_ref, ex_ref)
    acc_ref[...] = jnp.zeros_like(acc_ref)
    norm_ref[...] = jnp.zeros_like(norm_ref)

    def shift(step, slot):
        for tile in range(CHUNK // LANE):
            here = pl.ds(pl.multiple_of(step * CHUNK + tile * LANE, LANE), LANE)
            inverse = jnp.broadcast_to(inv_ref[0:1, here], (8, LANE))
            cosine = jnp.broadcast_to(cos_ref[:, here][:, None, :], (TR, O, LANE))
            sine = jnp.broadcast_to(sin_ref[:, here][:, None, :], (TR, O, LANE))
            start = 2 * tile * LANE
            for k in range(K):
                real = (nat_ref[k * 16 : k * 16 + 8, here] * inverse)[None]
                imag = (nat_ref[k * 16 + 8 : k * 16 + 16, here] * inverse)[None]
                rows = slice(k * 64, k * 64 + 64)
                shift_ref[slot, rows, start : start + LANE] = (
                    (real * cosine - imag * sine).reshape(TR * O, LANE).astype(jnp.bfloat16)
                )
                shift_ref[slot, rows, start + LANE : start + 2 * LANE] = (
                    (real * sine + imag * cosine).reshape(TR * O, LANE).astype(jnp.bfloat16)
                )
        lanes = pl.ds(pl.multiple_of(step * CHUNK, LANE), CHUNK)
        table = table_ref[0, :, lanes]
        powers = []
        for k in range(K):
            real = nat_ref[k * 16 : k * 16 + 8, lanes]
            imag = nat_ref[k * 16 + 8 : k * 16 + 16, lanes]
            powers.append(real * real + imag * imag)
        power = jnp.concatenate(powers, axis=0)
        ctf_power = table * table * inv_ref[0:1, lanes]
        norm_ref[...] += mm(power, ctf_power, ((1,), (1,)), lax.Precision.HIGHEST)

    def multiply(step, slot):
        acc_ref[...] += mm(shift_ref[slot], w_ref[step], ((1,), (1,)))

    shift(0, 0)

    def body(j, carry):
        weight_copy(w_hbm, w_ref, sem_ref, 2 * j).wait()
        weight_copy(w_hbm, w_ref, sem_ref, 2 * j + 1).wait()
        shift(2 * j + 1, 1)
        multiply(2 * j, 0)
        shift(2 * j + 2, 0)
        multiply(2 * j + 1, 1)
        return carry

    lax.fori_loop(0, STEPS // 2, body, 0)
    weight_copy(w_hbm, w_ref, sem_ref, STEPS - 1).wait()
    multiply(STEPS - 1, 0)

    wide = K * TR * O
    row = iota((wide, K * O), 0)
    widen = (iota((wide, K * O), 1) == (row // (TR * O)) * O + row % O).astype(jnp.float32)
    norm_wide = mm(widen, norm_ref[...], precision=lax.Precision.HIGHEST)
    onehot3 = onehot_rows(group_ref[...]).astype(jnp.bfloat16)
    scores = acc_ref[...] - 0.5 * mm(split3(norm_wide, 1), onehot3)
    orient = iota((wide, NP), 0) % O
    mask = orient_ref[0:1, :] == orient
    for n in range(1, 4):
        mask = mask | (orient_ref[n : n + 1, :] == orient)
    top = jnp.max(jnp.where(mask, scores, -jnp.inf), axis=0, keepdims=True)
    expo = jnp.exp(jnp.where(mask, scores - top, -jnp.inf))
    total = jnp.sum(expo, axis=0, keepdims=True)
    live = (iota((1, NP), 1) < pos_ref[3]).astype(jnp.float32)
    weights = expo / total * live
    rounded = weights.astype(jnp.bfloat16)
    for cls in range(2):
        for color, out in ((0, left_ref), (1, right_ref)):
            k = cls * 4 + color * 2
            out[cls * 128 : cls * 128 + 128, :] = rounded[k * 64 : k * 64 + 128, :]
    back_body(
        0, pos_ref, left_ref, w_ref, lambda step: None, cos_ref, sin_ref, (p0, p1, p2, p3),
        slab_ref, sum_ref, ex_ref,
    )


def order_kernel(left_ref, right_ref, post_ref):
    wide = K * TR * O
    row, col = iota((wide, wide), 0), iota((wide, wide), 1)
    target = (row // (TR * O)) * (TR * O) + (row % O) * TR + (row // O) % TR
    order = (col == target).astype(jnp.float32).astype(jnp.bfloat16)
    rows = []
    for cls in range(2):
        for ref in (left_ref, right_ref):
            rows.append(ref[cls * 128 : cls * 128 + 128, :].astype(jnp.float32))
    turned = jnp.concatenate(rows, axis=0).T.astype(jnp.bfloat16)
    post_ref[0] = mm(turned, order).astype(jnp.bfloat16)


def order_posterior(left, right):
    return pl.pallas_call(
        order_kernel,
        out_shape=jax.ShapeDtypeStruct((1, NP, K * TR * O), jnp.bfloat16),
        name="order_posterior",
    )(left, right)


SMEM = pl.BlockSpec(memory_space=pltpu.SMEM)
VMEM = pl.BlockSpec(memory_space=pltpu.VMEM)
ANY = pl.BlockSpec(memory_space=pl.ANY)


def score(pos, a, b, weighted, table, inverse, cosine, sine, group_row, orient):
    wide = K * O * TR
    return pl.pallas_call(
        score_kernel,
        in_specs=[SMEM] + [VMEM] * 8 + [ANY] + [VMEM] * 6,
        out_specs=[VMEM] * 6,
        scratch_shapes=[
            pltpu.VMEM((128, FC), jnp.float32),
            pltpu.VMEM((256, LANE), jnp.float32),
            pltpu.VMEM((2, wide, 2 * CHUNK), jnp.bfloat16),
            pltpu.VMEM((wide, NP), jnp.float32),
            pltpu.VMEM((K * O, G), jnp.float32),
            pltpu.VMEM((STEPS, NP, 2 * CHUNK), jnp.bfloat16),
            pltpu.SemaphoreType.DMA((STEPS,)),
            pltpu.VMEM((64, FC), jnp.float32),
            pltpu.VMEM((2, NP, 2 * CHUNK), jnp.float32),
        ],
        out_shape=[
            jax.ShapeDtypeStruct((wide // 2, NP), jnp.bfloat16),
            jax.ShapeDtypeStruct((wide // 2, NP), jnp.bfloat16),
        ]
        + [jax.ShapeDtypeStruct((4, ROWS, LANE), jnp.bfloat16)] * 4,
        compiler_params=pltpu.CompilerParams(vmem_limit_bytes=VMEM_LIMIT),
        name="score",
    )(pos, *a, *b, weighted, table, inverse, cosine, sine, group_row, orient)


def back_body(
    color, pos_ref, post_ref, w_ref, wait, cos_ref, sin_ref, outs, slab_ref, sum_ref, ex_ref
):
    def multiply(step, slot):
        sum_ref[slot] = mm(post_ref[...], w_ref[step])

    def combine(step, slot):
        for tile in range(CHUNK // LANE):
            here = pl.ds(pl.multiple_of(step * CHUNK + tile * LANE, LANE), LANE)
            cosine = jnp.broadcast_to(cos_ref[:, here][:, None, :], (TR, O, LANE))
            sine = jnp.broadcast_to(sin_ref[:, here][:, None, :], (TR, O, LANE))
            start = 2 * tile * LANE
            for k in range(4):
                rows = slice(k * 64, k * 64 + 64)
                real = sum_ref[slot, rows, start : start + LANE].reshape(TR, O, LANE)
                imag = sum_ref[slot, rows, start + LANE : start + 2 * LANE].reshape(TR, O, LANE)
                slab_ref[k * 16 : k * 16 + 8, here] = jnp.sum(
                    real * cosine + imag * sine, axis=0
                )
                slab_ref[k * 16 + 8 : k * 16 + 16, here] = jnp.sum(
                    imag * cosine - real * sine, axis=0
                )

    wait(0)
    multiply(0, 0)

    def body(j, carry):
        wait(2 * j + 1)
        wait(2 * j + 2)
        multiply(2 * j + 1, 1)
        combine(2 * j, 0)
        multiply(2 * j + 2, 0)
        combine(2 * j + 1, 1)
        return carry

    lax.fori_loop(0, STEPS // 2, body, 0)
    combine(STEPS - 1, 0)

    lane = iota((32, LANE), 1)
    for cls in range(2):
        rows = slice(cls * 32, cls * 32 + 32)
        tails = jnp.zeros((32, LANE), jnp.float32)
        for t in range(1, TILES):
            tails = jnp.where(lane // 2 == t - 1, slab_ref[rows, t * LANE : (t + 1) * LANE], tails)
        tails = tails.astype(jnp.bfloat16)
        total = jnp.zeros((64, LANE), jnp.float32)
        for u in range(2):
            pick = (iota((64, LANE), 1) == 2 * iota((64, LANE), 0) + u).astype(jnp.float32)
            column = mm(pick.astype(jnp.bfloat16), tails, ((1,), (1,)))
            spread = (iota((32, LANE), 1) == 2 * iota((32, LANE), 0) + u).astype(jnp.float32)
            total += mm(column.astype(jnp.bfloat16), spread.astype(jnp.bfloat16))
        ex_ref[cls * 64 : cls * 64 + 64, :] = total
    for near, out in enumerate(outs):

        def pack(far, carry, near=near, out=out):
            cls, chunks = sources(pos_ref, near, far, color)
            rows = pl.ds(pl.multiple_of(cls * 32, 32), 32)
            tails = []
            for slot, j in enumerate(chunks):
                here = pl.ds(pl.multiple_of(j * LANE, LANE), LANE)
                after = pl.ds(pl.multiple_of((j + 1) * LANE, LANE), LANE)
                both = jnp.where(lane >= 2 * j, slab_ref[rows, here], slab_ref[rows, after])
                main = pltpu.roll(both, LANE - 2 * j, 1)
                tails.append(ex_ref[pl.ds(cls * 64 + j, 1), :])
                out[far, slot * 32 : slot * 32 + 32, :] = main.astype(jnp.bfloat16)
            out[far, 256:264, :] = jnp.concatenate(tails, axis=0).astype(jnp.bfloat16)
            return carry

        lax.fori_loop(0, 4, pack, 0)


def back_kernel(
    pos_ref, post_ref, w_hbm, cos_ref, sin_ref, p0, p1, p2, p3,
    slab_ref, sum_ref, ex_ref, w_ref, sem_ref,
):
    for step in range(STEPS):
        weight_copy(w_hbm, w_ref, sem_ref, step).start()

    def wait(step):
        weight_copy(w_hbm, w_ref, sem_ref, step).wait()

    back_body(
        1, pos_ref, post_ref, w_ref, wait, cos_ref, sin_ref, (p0, p1, p2, p3),
        slab_ref, sum_ref, ex_ref,
    )


def project_back(pos, post, weighted, cosine, sine):
    return pl.pallas_call(
        back_kernel,
        in_specs=[SMEM, VMEM, ANY] + [VMEM] * 2,
        out_specs=[VMEM] * 4,
        scratch_shapes=[
            pltpu.VMEM((64, FC), jnp.float32),
            pltpu.VMEM((2, NP, 2 * CHUNK), jnp.float32),
            pltpu.VMEM((128, LANE), jnp.float32),
            pltpu.VMEM((STEPS, NP, 2 * CHUNK), jnp.bfloat16),
            pltpu.SemaphoreType.DMA((STEPS,)),
        ],
        out_shape=[jax.ShapeDtypeStruct((4, ROWS, LANE), jnp.bfloat16)] * 4,
        compiler_params=pltpu.CompilerParams(vmem_limit_bytes=VMEM_LIMIT),
        name="project_back",
    )(pos, post, weighted, cosine, sine)


def finish_kernel(own_ref, partner_ref, slab_ref, product_ref):
    lane = iota((8, LANE), 1)
    sub = iota((8, LANE), 0)

    def tails(row, group):
        first = 2 * (group * 8 + sub)
        wide = jnp.broadcast_to(row, (8, LANE))
        one = jnp.sum(jnp.where(lane == first, wide, 0.0), axis=1, keepdims=True)
        two = jnp.sum(jnp.where(lane == first + 1, wide, 0.0), axis=1, keepdims=True)
        return jnp.concatenate([one, two], axis=1)

    for color in range(2):
        base = color * 32
        own_row = own_ref[64 + color : 65 + color, :]
        partner_row = partner_ref[64:72, :].astype(jnp.float32)[color : color + 1]
        for kl in range(2):
            k = color * 2 + kl
            main, edge = 0.0, 0.0
            for c in range(2):
                group = kl * 2 + c
                rows = slice(base + group * 8, base + group * 8 + 8)
                own = own_ref[rows, :]
                own_tail = tails(own_row, group)
                slab_ref[0, k, :, c, 0:LANE] = own
                slab_ref[0, k, :, c, LANE : LANE + 2] = own_tail
                main += own * partner_ref[rows, :].astype(jnp.float32)
                edge += own_tail * tails(partner_row, group)
            product_ref[0, k, :, 0:LANE] = main
            product_ref[0, k, :, LANE : LANE + 2] = edge


def finish(own, partner):
    return pl.pallas_call(
        finish_kernel,
        out_shape=(
            jax.ShapeDtypeStruct((1, 4, O, 2, 130), jnp.float32),
            jax.ShapeDtypeStruct((1, 4, O, 130), jnp.float32),
        ),
        name="finish",
    )(own, partner)


def regroup_kernel(own_ref, got_ref, left_ref, right_ref):
    tails = ([], [])
    for slot in range(NZ):
        ref = own_ref if slot < 4 else got_ref
        last = ref[slot % 4, 64:72, :].astype(jnp.float32)
        for color, out in ((0, left_ref), (1, right_ref)):
            out[0, slot * 32 : slot * 32 + 32, :] = ref[slot % 4, color * 32 : color * 32 + 32, :]
            tails[color].append(last[color : color + 1])
    left_ref[0, 256:264, :] = jnp.concatenate(tails[0], axis=0).astype(jnp.bfloat16)
    right_ref[0, 256:264, :] = jnp.concatenate(tails[1], axis=0).astype(jnp.bfloat16)


def regroup(own, got):
    shape = jax.ShapeDtypeStruct((1, ROWS, LANE), jnp.bfloat16)
    return pl.pallas_call(regroup_kernel, out_shape=(shape, shape), name="regroup")(own, got)


def ungroup_kernel(l0_ref, l1_ref, r0_ref, r1_ref, keep_ref, send_ref):
    sub = iota((8, LANE), 0)
    tails = []
    for first, second in ((l0_ref, l1_ref), (r0_ref, r1_ref)):
        tails.append(first[0, 256:264, :] + second[0, 256:264, :].astype(jnp.float32))
    for slot in range(NZ):
        parts = []
        rows = slice(slot * 32, slot * 32 + 32)
        for first, second in ((l0_ref, l1_ref), (r0_ref, r1_ref)):
            parts.append(first[0, rows, :] + second[0, rows, :].astype(jnp.float32))
        left, right = tails[0][slot : slot + 1], tails[1][slot : slot + 1]
        parts.append(jnp.where(sub == 0, left, jnp.where(sub == 1, right, 0.0)))
        value = jnp.concatenate(parts, axis=0)
        if slot < 4:
            keep_ref[slot] = value
        else:
            send_ref[slot - 4] = value.astype(jnp.bfloat16)


def ungroup(l0, l1, r0, r1):
    return pl.pallas_call(
        ungroup_kernel,
        out_shape=(
            jax.ShapeDtypeStruct((4, 72, LANE), jnp.float32),
            jax.ShapeDtypeStruct((4, 72, LANE), jnp.bfloat16),
        ),
        name="ungroup",
    )(l0, l1, r0, r1)


def added(parts):
    total = parts[0].astype(jnp.float32)
    for part in parts[1:]:
        total = total + part.astype(jnp.float32)
    return total


def run(images, projections, ctf_table, ctf_group, orient_ids, trans_ids, inv_sigma, counts):
    cls, img = lax.axis_index("cls"), lax.axis_index("img")
    pos = jnp.stack(
        [img % 4, 2 * (img // 32) + cls, (img // 4) % 8, counts[0, 0]]
    ).astype(jnp.int32)
    cosine, sine = phases(trans_ids[0], FC)
    weighted = weight_images(images, ctf_table, ctf_group)

    along = pack_sections(projections)[None]
    for odd in (-1, 1):
        along = jnp.concatenate([along, trade_z(along, odd)])
    got = trade_z(along, -3)
    left, right = regroup(along, got)
    for mask in (1, 3):
        left = jnp.concatenate([left, trade(left, my=mask)])
        right = jnp.concatenate([right, trade(right, mx=mask)])
    lefts, rights = [left], [right]
    for mask in GRAY[1:]:
        lefts.append(trade(left, mx=mask))
    for mask in GRAY[1:]:
        rights.append(trade(right, my=mask))

    post_left, post_right, *pieces = score(
        pos, lefts, rights, weighted, ctf_table, inv_sigma, cosine, sine, ctf_group, orient_ids[0].T
    )

    left = added([pieces[0]] + [trade(pieces[d], mx=GRAY[d]) for d in range(1, 4)])
    pieces = project_back(pos, post_right, weighted, cosine, sine)
    parts = [pieces[0]]
    for d in range(1, 4):
        parts.append(trade(pieces[d], my=GRAY[d]))
    right = added(parts)
    posterior = order_posterior(post_left, post_right)
    left = added([left[:2], trade(left[2:].astype(jnp.bfloat16), my=3)])
    right = added([right[:2], trade(right[2:].astype(jnp.bfloat16), mx=3)])
    left_got = trade(left[1:].astype(jnp.bfloat16), my=1)
    right_got = trade(right[1:].astype(jnp.bfloat16), mx=1)
    own, sent = ungroup(left, left_got, right, right_got)
    own = own + trade_z(sent, -3).astype(jnp.float32)
    for odd, size in ((1, 2), (-1, 1)):
        own = added([own[:size], trade_z(own[size:].astype(jnp.bfloat16), odd)])
    own = own[0]
    partner = lax.ppermute(own.astype(jnp.bfloat16), "half", [(0, 1), (1, 0)])
    slab, product = finish(own, partner)
    return (posterior, slab, product)


def solution(mesh):
    return jax.shard_map(
        run,
        mesh=mesh,
        in_specs=(
            P("half", ("cls", "img"), None, None),
            P("half", "cls", None, None, "img"),
            P("half", None, None),
            P("half", ("cls", "img")),
            P("half", ("cls", "img"), None),
            P("half", None),
            P("half", None),
            P("half", ("cls", "img")),
        ),
        out_specs=(
            P("half", ("cls", "img"), None),
            P("half", "cls", None, None, "img"),
            P("half", "cls", None, "img"),
        ),
        check_vma=False,
    )
```

```python
import math

import jax
import jax.numpy as jnp
from jax import lax
from jax.experimental import pallas as pl
from jax.experimental.pallas import tpu as pltpu
from jax.sharding import PartitionSpec as P


K = 8
BOX = 128
O = 8
TR = 8
TGRID = 5
FC = 8320
G = 32
NP = 256
LANE = 128
TILES = FC // LANE
CHUNK = 640
STEPS = FC // CHUNK
PART = 1664
ROWS = 40
NX, NY, NZ = 4, 4, 8
GRAY = (0, 1, 3, 2)
Z_ORDER = (0, -1, 1, 2, -3, -2, -4, -5)
PAIR = ("cls", "img")
VMEM_LIMIT = 56 * 1024 * 1024


def place(index):
    cls, img = divmod(index, 64)
    y_hi, rest = divmod(img, 32)
    z, x = divmod(rest, 4)
    return x, 2 * y_hi + cls, z


def flat(x, y, z):
    x, y, z = x % NX, y % NY, z % NZ
    return (y % 2) * 64 + (y // 2) * 32 + z * 4 + x


def trade(value, mx=0, my=0):
    pairs = []
    for index in range(NX * NY * NZ):
        x, y, z = place(index)
        pairs.append((index, flat(x ^ mx, y ^ my, z)))
    return lax.ppermute(value, PAIR, pairs)


def trade_z(value, odd):
    pairs = []
    for index in range(NX * NY * NZ):
        x, y, z = place(index)
        pairs.append((index, flat(x, y, z + odd if z % 2 else z - odd)))
    return lax.ppermute(value, PAIR, pairs)


def sources(pos_ref, near, far, color):
    dx, dy = (near, far) if color == 0 else (far, near)
    x = pos_ref[0] ^ (dx ^ (dx >> 1))
    y = pos_ref[1] ^ (dy ^ (dy >> 1))
    sign = 2 * (pos_ref[2] % 2) - 1
    start = (y // 2) * 32 + x
    return y % 2, [start + ((pos_ref[2] + sign * dz) & 7) * 4 for dz in Z_ORDER]


def phases(trans_list, count):
    half_width = BOX // 2 + 1
    freq_index = jnp.arange(count, dtype=jnp.int32)
    row_index = freq_index // half_width
    col_index = freq_index % half_width
    wave_x = (row_index - BOX * (row_index >= BOX // 2).astype(jnp.int32)).astype(jnp.float32)
    wave_y = col_index.astype(jnp.float32)
    shift_x = (trans_list % TGRID - TGRID // 2).astype(jnp.float32)
    shift_y = (trans_list // TGRID - TGRID // 2).astype(jnp.float32)
    angle = (
        2.0
        * math.pi
        / BOX
        * (shift_x[:, None] * wave_x[None, :] + shift_y[:, None] * wave_y[None, :])
    )
    return (jnp.cos(angle), jnp.sin(angle))


def iota(shape, dim):
    return lax.broadcasted_iota(jnp.int32, shape, dim)


def split3(value, axis=0):
    high = value.astype(jnp.bfloat16)
    rest = value - high.astype(jnp.float32)
    mid = rest.astype(jnp.bfloat16)
    low = (rest - mid.astype(jnp.float32)).astype(jnp.bfloat16)
    return jnp.concatenate([high, mid, low], axis=axis)


def mm(left, right, dims=((1,), (0,)), precision=None):
    return lax.dot_general(
        left, right, (dims, ((), ())), precision=precision, preferred_element_type=jnp.float32
    )


def pack_kernel(p_ref, out_ref):
    lane = iota((8, LANE), 1)
    sub = iota((8, LANE), 0)
    for color in range(2):
        base = color * ROWS
        extra = jnp.zeros((8, LANE), jnp.float32)
        for kl in range(2):
            for c in range(2):
                rows = p_ref[0, color * 2 + kl, :, c, :].astype(jnp.float32)
                group = kl * 2 + c
                start = base + group * 8
                out_ref[0, start : start + 8, :] = rows[:, :LANE].astype(jnp.bfloat16)
                first = 2 * (group * 8 + sub)
                extra += jnp.where(lane == first, rows[:, LANE : LANE + 1], 0.0)
                extra += jnp.where(lane == first + 1, rows[:, LANE + 1 : LANE + 2], 0.0)
        row = jnp.sum(extra, axis=0, keepdims=True)
        tail = jnp.broadcast_to(row, (8, LANE))
        out_ref[0, base + 32 : base + 40, :] = tail.astype(jnp.bfloat16)


def pack_sections(projections):
    shape = jax.ShapeDtypeStruct((1, 2 * ROWS, LANE), jnp.bfloat16)
    return pl.pallas_call(pack_kernel, out_shape=shape, name="pack_sections")(projections)


def onehot_rows(group_row):
    onehot = (iota((G, NP), 0) == group_row).astype(jnp.float32)
    return jnp.concatenate([onehot, onehot, onehot], axis=0)


def weight_kernel(image_ref, table_ref, group_ref, out_ref, ctf_ref, onehot_ref):
    @pl.when(pl.program_id(0) == 0)
    def _():
        onehot_ref[...] = onehot_rows(group_ref[...]).T.astype(jnp.bfloat16)

    ctf_ref[...] = mm(onehot_ref[...], split3(table_ref[0]))

    def body(i, carry):
        rows = pl.ds(pl.multiple_of(i * 16, 16), 16)
        for c in range(2):
            value = image_ref[0, rows, c, :].astype(jnp.float32)
            value = (ctf_ref[rows, :] * value).astype(jnp.bfloat16)
            for tile in range(PART // LANE):
                start = (2 * tile + c) * LANE
                out_ref[rows, start : start + LANE] = value[:, tile * LANE : (tile + 1) * LANE]
        return carry

    lax.fori_loop(0, NP // 16, body, 0)


def weight_images(images, table, group_row):
    return pl.pallas_call(
        weight_kernel,
        grid=(FC // PART,),
        in_specs=[
            pl.BlockSpec((1, NP, 2, PART), lambda j: (0, 0, 0, j)),
            pl.BlockSpec((1, G, PART), lambda j: (0, 0, j)),
            pl.BlockSpec((1, NP), lambda j: (0, 0)),
        ],
        out_specs=pl.BlockSpec((NP, 2 * PART), lambda j: (0, j)),
        out_shape=jax.ShapeDtypeStruct((NP, 2 * FC), jnp.bfloat16),
        scratch_shapes=[
            pltpu.VMEM((NP, PART), jnp.float32),
            pltpu.VMEM((NP, 3 * G), jnp.bfloat16),
        ],
        compiler_params=pltpu.CompilerParams(vmem_limit_bytes=VMEM_LIMIT),
        name="weight_images",
    )(images, table, group_row)


def weight_copy(w_hbm, w_ref, sem_ref, step):
    lanes = pl.ds(pl.multiple_of(step * (2 * CHUNK), LANE), 2 * CHUNK)
    return pltpu.make_async_copy(w_hbm.at[:, lanes], w_ref.at[step], sem_ref.at[step])


def unpack_sections(pos_ref, a_refs, b_refs, nat_ref, ex_ref):
    lane = iota((32, LANE), 1)
    for color, refs in ((0, a_refs), (1, b_refs)):
        for near in range(4):
            ref = refs[near]

            def body(far, carry, ref=ref, near=near, color=color):
                cls, chunks = sources(pos_ref, near, far, color)
                rows = pl.ds(pl.multiple_of(cls * 64 + color * 32, 32), 32)
                for slot, j in enumerate(chunks):
                    piece = ref[far, slot].astype(jnp.float32)
                    turned = pltpu.roll(piece[:32], 2 * j, 1)
                    here = pl.ds(pl.multiple_of(j * LANE, LANE), LANE)
                    after = pl.ds(pl.multiple_of((j + 1) * LANE, LANE), LANE)
                    pltpu.store(nat_ref.at[rows, here], turned, mask=lane >= 2 * j)
                    pltpu.store(nat_ref.at[rows, after], turned, mask=lane < 2 * j)
                    ex_ref[pl.ds(cls * 128 + color * 64 + j, 1), :] = piece[32:33]
                return carry

            lax.fori_loop(0, 4, body, 0)
    for cls in range(2):
        for color in range(2):
            start = cls * 128 + color * 64
            extra = ex_ref[start : start + 64, :].astype(jnp.bfloat16)
            total = jnp.zeros((32, LANE), jnp.float32)
            for u in range(2):
                pick = (iota((32, LANE), 1) == 2 * iota((32, LANE), 0) + u).astype(jnp.float32)
                column = mm(pick.astype(jnp.bfloat16), extra, ((1,), (1,)))
                spread = (iota((64, LANE), 1) == 2 * iota((64, LANE), 0) + u).astype(jnp.float32)
                total += mm(column.astype(jnp.bfloat16), spread.astype(jnp.bfloat16))
            rows = slice(cls * 64 + color * 32, cls * 64 + color * 32 + 32)
            for t in range(1, TILES):
                here = slice(t * LANE, (t + 1) * LANE)
                pltpu.store(nat_ref.at[rows, here], total, mask=lane // 2 == t - 1)


def score_kernel(
    pos_ref, a0, a1, a2, a3, b0, b1, b2, b3, w_hbm, table_ref, inv_ref, cos_ref, sin_ref,
    group_ref, orient_ref, left_ref, right_ref, p0, p1, p2, p3,
    nat_ref, ex_ref, shift_ref, acc_ref, norm_ref, w_ref, sem_ref, slab_ref, sum_ref,
):
    for step in range(STEPS):
        weight_copy(w_hbm, w_ref, sem_ref, step).start()
    unpack_sections(pos_ref, (a0, a1, a2, a3), (b0, b1, b2, b3), nat_ref, ex_ref)
    acc_ref[...] = jnp.zeros_like(acc_ref)
    norm_ref[...] = jnp.zeros_like(norm_ref)

    def shift(step, slot):
        for tile in range(CHUNK // LANE):
            here = pl.ds(pl.multiple_of(step * CHUNK + tile * LANE, LANE), LANE)
            inverse = jnp.broadcast_to(inv_ref[0:1, here], (8, LANE))
            cosine = jnp.broadcast_to(cos_ref[:, here][:, None, :], (TR, O, LANE))
            sine = jnp.broadcast_to(sin_ref[:, here][:, None, :], (TR, O, LANE))
            start = 2 * tile * LANE
            for k in range(K):
                real = (nat_ref[k * 16 : k * 16 + 8, here] * inverse)[None]
                imag = (nat_ref[k * 16 + 8 : k * 16 + 16, here] * inverse)[None]
                rows = slice(k * 64, k * 64 + 64)
                shift_ref[slot, rows, start : start + LANE] = (
                    (real * cosine - imag * sine).reshape(TR * O, LANE).astype(jnp.bfloat16)
                )
                shift_ref[slot, rows, start + LANE : start + 2 * LANE] = (
                    (real * sine + imag * cosine).reshape(TR * O, LANE).astype(jnp.bfloat16)
                )
        lanes = pl.ds(pl.multiple_of(step * CHUNK, LANE), CHUNK)
        table = table_ref[0, :, lanes]
        powers = []
        for k in range(K):
            real = nat_ref[k * 16 : k * 16 + 8, lanes]
            imag = nat_ref[k * 16 + 8 : k * 16 + 16, lanes]
            powers.append(real * real + imag * imag)
        power = jnp.concatenate(powers, axis=0)
        ctf_power = table * table * inv_ref[0:1, lanes]
        norm_ref[...] += mm(power, ctf_power, ((1,), (1,)), lax.Precision.HIGHEST)

    def multiply(step, slot):
        acc_ref[...] += mm(shift_ref[slot], w_ref[step], ((1,), (1,)))

    shift(0, 0)

    def body(j, carry):
        weight_copy(w_hbm, w_ref, sem_ref, 2 * j).wait()
        weight_copy(w_hbm, w_ref, sem_ref, 2 * j + 1).wait()
        shift(2 * j + 1, 1)
        multiply(2 * j, 0)
        shift(2 * j + 2, 0)
        multiply(2 * j + 1, 1)
        return carry

    lax.fori_loop(0, STEPS // 2, body, 0)
    weight_copy(w_hbm, w_ref, sem_ref, STEPS - 1).wait()
    multiply(STEPS - 1, 0)

    wide = K * TR * O
    row = iota((wide, K * O), 0)
    widen = (iota((wide, K * O), 1) == (row // (TR * O)) * O + row % O).astype(jnp.float32)
    norm_wide = mm(widen, norm_ref[...], precision=lax.Precision.HIGHEST)
    onehot3 = onehot_rows(group_ref[...]).astype(jnp.bfloat16)
    scores = acc_ref[...] - 0.5 * mm(split3(norm_wide, 1), onehot3)
    orient = iota((wide, NP), 0) % O
    mask = orient_ref[0:1, :] == orient
    for n in range(1, 4):
        mask = mask | (orient_ref[n : n + 1, :] == orient)
    top = jnp.max(jnp.where(mask, scores, -jnp.inf), axis=0, keepdims=True)
    expo = jnp.exp(jnp.where(mask, scores - top, -jnp.inf))
    total = jnp.sum(expo, axis=0, keepdims=True)
    live = (iota((1, NP), 1) < pos_ref[3]).astype(jnp.float32)
    weights = expo / total * live
    rounded = weights.astype(jnp.bfloat16)
    for cls in range(2):
        for color, out in ((0, left_ref), (1, right_ref)):
            k = cls * 4 + color * 2
            out[cls * 128 : cls * 128 + 128, :] = rounded[k * 64 : k * 64 + 128, :]
    back_body(
        0, pos_ref, left_ref, w_ref, lambda step: None, cos_ref, sin_ref, (p0, p1, p2, p3),
        slab_ref, sum_ref, ex_ref,
    )


def order_kernel(left_ref, right_ref, post_ref):
    wide = K * TR * O
    row, col = iota((wide, wide), 0), iota((wide, wide), 1)
    target = (row // (TR * O)) * (TR * O) + (row % O) * TR + (row // O) % TR
    order = (col == target).astype(jnp.float32).astype(jnp.bfloat16)
    rows = []
    for cls in range(2):
        for ref in (left_ref, right_ref):
            rows.append(ref[cls * 128 : cls * 128 + 128, :].astype(jnp.float32))
    turned = jnp.concatenate(rows, axis=0).T.astype(jnp.bfloat16)
    post_ref[0] = mm(turned, order).astype(jnp.bfloat16)


def order_posterior(left, right):
    return pl.pallas_call(
        order_kernel,
        out_shape=jax.ShapeDtypeStruct((1, NP, K * TR * O), jnp.bfloat16),
        name="order_posterior",
    )(left, right)


SMEM = pl.BlockSpec(memory_space=pltpu.SMEM)
VMEM = pl.BlockSpec(memory_space=pltpu.VMEM)
ANY = pl.BlockSpec(memory_space=pl.ANY)


def score(pos, a, b, weighted, table, inverse, cosine, sine, group_row, orient):
    wide = K * O * TR
    return pl.pallas_call(
        score_kernel,
        in_specs=[SMEM] + [VMEM] * 8 + [ANY] + [VMEM] * 6,
        out_specs=[VMEM] * 6,
        scratch_shapes=[
            pltpu.VMEM((128, FC), jnp.float32),
            pltpu.VMEM((256, LANE), jnp.float32),
            pltpu.VMEM((2, wide, 2 * CHUNK), jnp.bfloat16),
            pltpu.VMEM((wide, NP), jnp.float32),
            pltpu.VMEM((K * O, G), jnp.float32),
            pltpu.VMEM((STEPS, NP, 2 * CHUNK), jnp.bfloat16),
            pltpu.SemaphoreType.DMA((STEPS,)),
            pltpu.VMEM((64, FC), jnp.float32),
            pltpu.VMEM((2, NP, 2 * CHUNK), jnp.float32),
        ],
        out_shape=[
            jax.ShapeDtypeStruct((wide // 2, NP), jnp.bfloat16),
            jax.ShapeDtypeStruct((wide // 2, NP), jnp.bfloat16),
        ]
        + [jax.ShapeDtypeStruct((4, NZ, ROWS, LANE), jnp.bfloat16)] * 4,
        compiler_params=pltpu.CompilerParams(vmem_limit_bytes=VMEM_LIMIT),
        name="score",
    )(pos, *a, *b, weighted, table, inverse, cosine, sine, group_row, orient)


def back_body(
    color, pos_ref, post_ref, w_ref, wait, cos_ref, sin_ref, outs, slab_ref, sum_ref, ex_ref
):
    def multiply(step, slot):
        sum_ref[slot] = mm(post_ref[...], w_ref[step])

    def combine(step, slot):
        for tile in range(CHUNK // LANE):
            here = pl.ds(pl.multiple_of(step * CHUNK + tile * LANE, LANE), LANE)
            cosine = jnp.broadcast_to(cos_ref[:, here][:, None, :], (TR, O, LANE))
            sine = jnp.broadcast_to(sin_ref[:, here][:, None, :], (TR, O, LANE))
            start = 2 * tile * LANE
            for k in range(4):
                rows = slice(k * 64, k * 64 + 64)
                real = sum_ref[slot, rows, start : start + LANE].reshape(TR, O, LANE)
                imag = sum_ref[slot, rows, start + LANE : start + 2 * LANE].reshape(TR, O, LANE)
                slab_ref[k * 16 : k * 16 + 8, here] = jnp.sum(
                    real * cosine + imag * sine, axis=0
                )
                slab_ref[k * 16 + 8 : k * 16 + 16, here] = jnp.sum(
                    imag * cosine - real * sine, axis=0
                )

    wait(0)
    multiply(0, 0)

    def body(j, carry):
        wait(2 * j + 1)
        wait(2 * j + 2)
        multiply(2 * j + 1, 1)
        combine(2 * j, 0)
        multiply(2 * j + 2, 0)
        combine(2 * j + 1, 1)
        return carry

    lax.fori_loop(0, STEPS // 2, body, 0)
    combine(STEPS - 1, 0)

    lane = iota((32, LANE), 1)
    for cls in range(2):
        rows = slice(cls * 32, cls * 32 + 32)
        tails = jnp.zeros((32, LANE), jnp.float32)
        for t in range(1, TILES):
            tails = jnp.where(lane // 2 == t - 1, slab_ref[rows, t * LANE : (t + 1) * LANE], tails)
        tails = tails.astype(jnp.bfloat16)
        total = jnp.zeros((64, LANE), jnp.float32)
        for u in range(2):
            pick = (iota((64, LANE), 1) == 2 * iota((64, LANE), 0) + u).astype(jnp.float32)
            column = mm(pick.astype(jnp.bfloat16), tails, ((1,), (1,)))
            spread = (iota((32, LANE), 1) == 2 * iota((32, LANE), 0) + u).astype(jnp.float32)
            total += mm(column.astype(jnp.bfloat16), spread.astype(jnp.bfloat16))
        ex_ref[cls * 64 : cls * 64 + 64, :] = total
    for near, out in enumerate(outs):

        def pack(far, carry, near=near, out=out):
            cls, chunks = sources(pos_ref, near, far, color)
            rows = pl.ds(pl.multiple_of(cls * 32, 32), 32)
            for slot, j in enumerate(chunks):
                here = pl.ds(pl.multiple_of(j * LANE, LANE), LANE)
                after = pl.ds(pl.multiple_of((j + 1) * LANE, LANE), LANE)
                both = jnp.where(lane >= 2 * j, slab_ref[rows, here], slab_ref[rows, after])
                main = pltpu.roll(both, LANE - 2 * j, 1)
                tail = ex_ref[pl.ds(cls * 64 + j, 1), :]
                out[far, slot, 0:32, :] = main.astype(jnp.bfloat16)
                out[far, slot, 32:40, :] = jnp.broadcast_to(tail, (8, LANE)).astype(jnp.bfloat16)
            return carry

        lax.fori_loop(0, 4, pack, 0)


def back_kernel(
    pos_ref, post_ref, w_hbm, cos_ref, sin_ref, p0, p1, p2, p3,
    slab_ref, sum_ref, ex_ref, w_ref, sem_ref,
):
    for step in range(STEPS):
        weight_copy(w_hbm, w_ref, sem_ref, step).start()

    def wait(step):
        weight_copy(w_hbm, w_ref, sem_ref, step).wait()

    back_body(
        1, pos_ref, post_ref, w_ref, wait, cos_ref, sin_ref, (p0, p1, p2, p3),
        slab_ref, sum_ref, ex_ref,
    )


def project_back(pos, post, weighted, cosine, sine):
    return pl.pallas_call(
        back_kernel,
        in_specs=[SMEM, VMEM, ANY, VMEM, VMEM],
        out_specs=[VMEM] * 4,
        scratch_shapes=[
            pltpu.VMEM((64, FC), jnp.float32),
            pltpu.VMEM((2, NP, 2 * CHUNK), jnp.float32),
            pltpu.VMEM((128, LANE), jnp.float32),
            pltpu.VMEM((STEPS, NP, 2 * CHUNK), jnp.bfloat16),
            pltpu.SemaphoreType.DMA((STEPS,)),
        ],
        out_shape=[jax.ShapeDtypeStruct((4, NZ, ROWS, LANE), jnp.bfloat16)] * 4,
        compiler_params=pltpu.CompilerParams(vmem_limit_bytes=VMEM_LIMIT),
        name="project_back",
    )(pos, post, weighted, cosine, sine)


def finish_kernel(own_ref, partner_ref, slab_ref, product_ref):
    lane = iota((8, LANE), 1)
    sub = iota((8, LANE), 0)

    def tails(row, group):
        first = 2 * (group * 8 + sub)
        wide = jnp.broadcast_to(row, (8, LANE))
        one = jnp.sum(jnp.where(lane == first, wide, 0.0), axis=1, keepdims=True)
        two = jnp.sum(jnp.where(lane == first + 1, wide, 0.0), axis=1, keepdims=True)
        return jnp.concatenate([one, two], axis=1)

    for color in range(2):
        base = color * ROWS
        own_row = own_ref[base + 32 : base + 33, :]
        partner_row = partner_ref[base + 32 : base + 40, :].astype(jnp.float32)[0:1]
        for kl in range(2):
            k = color * 2 + kl
            main, edge = 0.0, 0.0
            for c in range(2):
                group = kl * 2 + c
                rows = slice(base + group * 8, base + group * 8 + 8)
                own = own_ref[rows, :]
                own_tail = tails(own_row, group)
                slab_ref[0, k, :, c, 0:LANE] = own
                slab_ref[0, k, :, c, LANE : LANE + 2] = own_tail
                main += own * partner_ref[rows, :].astype(jnp.float32)
                edge += own_tail * tails(partner_row, group)
            product_ref[0, k, :, 0:LANE] = main
            product_ref[0, k, :, LANE : LANE + 2] = edge


def finish(own, partner):
    return pl.pallas_call(
        finish_kernel,
        out_shape=(
            jax.ShapeDtypeStruct((1, 4, O, 2, 130), jnp.float32),
            jax.ShapeDtypeStruct((1, 4, O, 130), jnp.float32),
        ),
        name="finish",
    )(own, partner)


def added(parts):
    total = parts[0].astype(jnp.float32)
    for part in parts[1:]:
        total = total + part.astype(jnp.float32)
    return total


def run(images, projections, ctf_table, ctf_group, orient_ids, trans_ids, inv_sigma, counts):
    cls, img = lax.axis_index("cls"), lax.axis_index("img")
    pos = jnp.stack(
        [img % 4, 2 * (img // 32) + cls, (img // 4) % 8, counts[0, 0]]
    ).astype(jnp.int32)
    cosine, sine = phases(trans_ids[0], FC)
    weighted = weight_images(images, ctf_table, ctf_group)

    along = pack_sections(projections)
    for odd in (-1, 1, -3):
        along = jnp.concatenate([along, trade_z(along, odd)])
    left, right = along[None, :, :ROWS], along[None, :, ROWS:]
    for mask in (1, 3):
        left = jnp.concatenate([left, trade(left, my=mask)])
        right = jnp.concatenate([right, trade(right, mx=mask)])
    lefts, rights = [left], [right]
    for mask in GRAY[1:]:
        lefts.append(trade(left, mx=mask))
    for mask in GRAY[1:]:
        rights.append(trade(right, my=mask))

    post_left, post_right, *pieces = score(
        pos, lefts, rights, weighted, ctf_table, inv_sigma, cosine, sine, ctf_group, orient_ids[0].T
    )

    left = added([pieces[0]] + [trade(pieces[d], mx=GRAY[d]) for d in range(1, 4)])
    pieces = project_back(pos, post_right, weighted, cosine, sine)
    parts = [pieces[0]]
    for d in range(1, 4):
        parts.append(trade(pieces[d], my=GRAY[d]))
    right = added(parts)
    posterior = order_posterior(post_left, post_right)
    for mask, size in ((3, 2), (1, 1)):
        left, right = left.astype(jnp.bfloat16), right.astype(jnp.bfloat16)
        left = added([left[:size], trade(left[size:], my=mask)])
        right = added([right[:size], trade(right[size:], mx=mask)])
    own = jnp.concatenate([left[0], right[0]], axis=1)
    for odd, size in ((-3, 4), (1, 2), (-1, 1)):
        own = own.astype(jnp.bfloat16)
        own = added([own[:size], trade_z(own[size:], odd)])
    own = own[0]
    partner = lax.ppermute(own.astype(jnp.bfloat16), "half", [(0, 1), (1, 0)])
    slab, product = finish(own, partner)
    return (posterior, slab, product)


def solution(mesh):
    return jax.shard_map(
        run,
        mesh=mesh,
        in_specs=(
            P("half", ("cls", "img"), None, None),
            P("half", "cls", None, None, "img"),
            P("half", None, None),
            P("half", ("cls", "img")),
            P("half", ("cls", "img"), None),
            P("half", None),
            P("half", None),
            P("half", ("cls", "img")),
        ),
        out_specs=(
            P("half", ("cls", "img"), None),
            P("half", "cls", None, None, "img"),
            P("half", "cls", None, "img"),
        ),
        check_vma=False,
    )
```
